256 devices in a mesh: section: 2 (over core), block: 16 (over y, x), dp: 8 (over z).
Axes of the slice: x: 4, y: 4, z: 8, core: 2. Of those that a mesh axis runs over, the one named last changes fastest.
Arguments:
- embeds: bfloat16 [16, 4096, 1024], P('dp', 'block'), parts along dimension 0, may hold values from -4 to 4
- wide_in: bfloat16 [2, 1024, 2304], P('section'), may hold values from -0.1875 to 0.1875
- rate_in: bfloat16 [2, 1024, 32], P('section'), may hold values from -0.375 to 0.375
- kernel: float32 [2, 4, 2304], P('section'), may hold values from -3 to 3
- kernel_bias: float32 [2, 2304], P('section'), may hold values from -0.5 to 0.5
- step_bias: float32 [2, 32], P('section'), may hold values from -12 to -1
- decay_log: float32 [2, 32], P('section'), may hold values from -2.3 to -0.7
- skip_gain: float32 [2, 32], P('section'), may hold values from 0.5 to 1.5
- norm_gain: float32 [2, 1024], P('section'), may hold values from 0.5 to 1.5
- inner_gain: float32 [2, 2048], P('section'), may hold values from 0.25 to 1.75
- proj_out: bfloat16 [2, 2048, 1024], P('section'), may hold values from -0.09375 to 0.09375
Outputs:
- hiddens: bfloat16 [2, 16, 4096, 1024], P('section', 'dp', 'block'), parts along dimension 1
The draws below stay inside these ranges and needn't reach their ends.
There are 8 independent parts, one for each index of `dp`. The reference program is written for one: setup_inputs(seed, part) draws one part's arguments, and reference() takes and returns one part's arrays. A program takes and returns all parts, laid end to end along the dimension named above; an argument that names none is the same for every part. Nothing has to cross between parts.
All inputs are finite; a program needn't handle non-finite values.
Results may differ from the reference program's by a relative error of at most 0.039.
Values may be sent and summed in bfloat16 or wider, within the bound.
A program may use at most 128 MiB of HBM per device.

```python
import jax
import jax.numpy as jnp
from jax import lax

D = 1024
H = 32
P_SIZE = 64
N = 128
KCONV = 4
TOK = 256
SEQS = 2
INNER = 2048
XBC = 2304
LAYERS = 2
LENGTH = 4096
N_BLOCK = 16


def draw_embeds(key, part):
    key_noise = jax.random.fold_in(key, 11)
    key_dir = jax.random.fold_in(key, 12)
    key_amp = jax.random.fold_in(key, 13)
    noise = jnp.clip(0.5 * jax.random.normal(key_noise, (SEQS, LENGTH, D), jnp.float32), -2.0, 2.0)
    direction = jnp.clip(jax.random.normal(key_dir, (D,), jnp.float32), -2.5, 2.5)
    amplitude = jax.random.uniform(key_amp, (SEQS, LENGTH // TOK), jnp.float32, -0.7, 0.7)
    offsets = jnp.repeat(amplitude, TOK, axis=1)
    return (noise + offsets[:, :, None] * direction[None, None, :]).astype(jnp.bfloat16)


def head_rates(key):
    decay_log = jax.random.uniform(jax.random.fold_in(key, 31), (LAYERS, H), jnp.float32, -2.3, -0.7)
    fraction = jax.random.uniform(jax.random.fold_in(key, 32), (LAYERS, H), jnp.float32)
    lowest = jnp.log(jnp.float32(1.0 / (64.0 * LENGTH)))
    highest = jnp.log(jnp.float32(1.0 / 48.0))
    effective = jnp.exp(lowest + fraction * (highest - lowest))
    step_size = effective * jnp.exp(-decay_log)
    return (decay_log, jnp.log(jnp.expm1(step_size)))


def draw_decay_log(key, part):
    return head_rates(key)[0]


def draw_step_bias(key, part):
    return head_rates(key)[1]


def shard_levels(key, dims, shards, low, high):
    def one(position, blocks):
        heights = jax.random.uniform(jax.random.fold_in(jax.random.fold_in(key, 6), position), (blocks,), jnp.float32, low / len(shards), high / len(shards))
        return jnp.repeat(jnp.exp(heights), dims[position] // blocks).reshape((-1,) + (1,) * (len(dims) - position - 1))

    loudness = one(*shards[0])
    for cut in shards[1:]:
        loudness = loudness * one(*cut)
    return loudness


def bell_draw(key, dims, spread, bound, cuts=(), kind=jnp.bfloat16):
    loudness = shard_levels(key, dims, cuts, -0.22, 0.18) if cuts else 1.0
    drawn = jax.random.normal(key, dims, jnp.float32) * spread * loudness
    return jnp.minimum(jnp.maximum(drawn, -bound), bound).astype(kind)


def setup_inputs(seed: int = 0, part: int = 0) -> dict:
    splits = jax.random.split(jax.random.key(seed), 12)
    part_keys = jax.random.split(jax.random.fold_in(splits[11], part), 12)
    embeds = draw_embeds(jax.random.fold_in(jax.random.fold_in(splits[11], part), 71), part)
    wide_in = bell_draw(splits[1], (LAYERS, D, XBC), D ** -0.5, 0.1875, ((0, 2),))
    rate_in = bell_draw(splits[2], (LAYERS, D, H), (D // 4) ** -0.5, 0.375, ((0, 2),))
    kernel = bell_draw(splits[3], (LAYERS, KCONV, XBC), KCONV ** -0.5, 3.0, ((0, 2),), jnp.float32)
    kernel_bias = jnp.clip(jax.random.uniform(splits[4], (LAYERS, XBC), jnp.float32, -0.5, 0.5) * shard_levels(splits[4], (LAYERS, XBC), ((0, 2),), -0.4, 0.0), -0.5, 0.5)
    step_bias = draw_step_bias(jax.random.fold_in(splits[11], 71), part)
    decay_log = draw_decay_log(jax.random.fold_in(splits[11], 71), part)
    skip_gain = jnp.clip(0.5 + 1.0 * jax.random.uniform(splits[7], (LAYERS, H), jnp.float32) ** shard_levels(splits[7], (LAYERS, H), ((0, 2),), -0.2, 0.2), 0.5, 1.5)
    norm_gain = jnp.clip(1.0 + 0.1 * jax.random.normal(splits[8], (LAYERS, D), jnp.float32), 0.5, 1.5)
    inner_gain = jnp.clip(0.25 + 1.5 * jax.random.uniform(splits[9], (LAYERS, INNER), jnp.float32) ** shard_levels(splits[9], (LAYERS, INNER), ((0, 2),), -0.2, 0.2), 0.25, 1.75)
    proj_out = bell_draw(splits[10], (LAYERS, INNER, D), (2 * INNER) ** -0.5, 0.09375, ((0, 2),))
    return dict(embeds=embeds, wide_in=wide_in, rate_in=rate_in, kernel=kernel, kernel_bias=kernel_bias, step_bias=step_bias, decay_log=decay_log, skip_gain=skip_gain, norm_gain=norm_gain, inner_gain=inner_gain, proj_out=proj_out)


def rms_scale(values, gain):
    return values * lax.rsqrt(lax.optimization_barrier(jnp.mean(values * values, axis=-1, keepdims=True)) + 1e-05) * gain

def run_layer(resid, params):
    wide_in, rate_in, kernel, kernel_bias, step_bias, decay_log, skip_gain, norm_gain, inner_gain, proj_out = params
    normed = rms_scale(resid.astype(jnp.float32), norm_gain).astype(jnp.bfloat16)
    xbc_raw = lax.optimization_barrier(jnp.dot(normed, wide_in, preferred_element_type=jnp.float32).astype(jnp.bfloat16))
    step_raw = jnp.dot(normed, rate_in, preferred_element_type=jnp.float32)
    padded = jnp.concatenate([jnp.zeros((KCONV - 1, XBC), jnp.bfloat16), xbc_raw], 0)
    convolved = kernel_bias
    for offset in range(KCONV):
        convolved = convolved + padded[offset:offset + LENGTH].astype(jnp.float32) * kernel[offset]
    active = lax.optimization_barrier(jax.nn.silu(convolved).astype(jnp.bfloat16))
    step = jax.nn.softplus(step_raw + step_bias)
    rate = jnp.exp(decay_log)
    positions = jnp.arange(TOK)
    causal = positions[:, None] >= positions[None, :]
    incoming = jnp.zeros((H, P_SIZE, N), jnp.float32)
    pieces = []
    for index in range(N_BLOCK):
        start = index * TOK
        values = active[start:start + TOK, :INNER]
        b_rows = active[start:start + TOK, INNER:INNER + N]
        c_rows = active[start:start + TOK, INNER + N:]
        step_here = step[start:start + TOK]
        cumul = jnp.cumsum(-step_here * rate, axis=0).T
        gaps = cumul[:, :, None] - cumul[:, None, :]
        decay = jnp.where(causal[None], jnp.exp(jnp.where(causal[None], gaps, 0.0)), 0.0)
        scores = jnp.dot(c_rows, b_rows.T, preferred_element_type=jnp.float32)
        mixing = lax.optimization_barrier((scores[None] * decay * step_here.T[:, None, :]).astype(jnp.bfloat16))
        heads_view = values.reshape(TOK, H, P_SIZE)
        diagonal_part = jnp.einsum('hij,jhp->ihp', mixing.astype(jnp.float32), heads_view.astype(jnp.float32))
        tail_weight = jnp.exp(cumul[:, -1:] - cumul) * step_here.T
        weighted = lax.optimization_barrier((heads_view.astype(jnp.float32) * tail_weight.T[:, :, None]).astype(jnp.bfloat16))
        block_state = jnp.einsum('ti,tn->in', weighted.reshape(TOK, INNER).astype(jnp.float32), b_rows.astype(jnp.float32)).reshape(H, P_SIZE, N)
        block_decay = jnp.exp(cumul[:, -1])
        carried = jnp.einsum('tn,in->ti', c_rows.astype(jnp.float32), incoming.reshape(INNER, N), precision=lax.Precision.HIGHEST)
        offdiag = carried.reshape(TOK, H, P_SIZE) * jnp.exp(cumul).T[:, :, None]
        total = diagonal_part + offdiag + heads_view.astype(jnp.float32) * skip_gain[None, :, None]
        pieces.append(total.reshape(TOK, INNER))
        incoming = block_decay[:, None, None] * incoming + block_state
    total = jnp.concatenate(pieces, 0)
    ynormed = rms_scale(total, inner_gain).astype(jnp.bfloat16)
    result = (resid.astype(jnp.float32) + jnp.dot(ynormed, proj_out, preferred_element_type=jnp.float32)).astype(jnp.bfloat16)
    return (result, result)

def reference(embeds, wide_in, rate_in, kernel, kernel_bias, step_bias, decay_log, skip_gain, norm_gain, inner_gain, proj_out):
    params = (wide_in, rate_in, kernel, kernel_bias, step_bias, decay_log, skip_gain, norm_gain, inner_gain, proj_out)

    def one_sequence(sequence):
        final, layers = lax.scan(run_layer, sequence, params)
        return layers
    stacked = lax.map(one_sequence, embeds)
    return jnp.transpose(stacked, (1, 0, 2, 3))
```

```python
import functools

import jax
import jax.numpy as jnp
from jax import lax
from jax.experimental import pallas as pl
from jax.experimental.pallas import tpu as pltpu
from jax.sharding import PartitionSpec as P

MESH = pl.DeviceIdType.MESH
F32, BF16 = jnp.float32, jnp.bfloat16
LOG2E = 1.4426950408889634
EPS = 1e-05
DECAY_ROWS = 16


def split2(x):
    hi = x.astype(BF16)
    return hi, (x - hi.astype(F32)).astype(BF16)


def dot(a, b):
    return jnp.dot(a, b, preferred_element_type=F32)


def dot_nt(a, b):
    return lax.dot_general(a, b, (((1,), (1,)), ((), ())), preferred_element_type=F32)


def kernel(
    blocks,
    emb, wide, rate, taps, tbias, sbias, dlog, skip, ngain, igain, proj,
    out,
    h, win, wo, rt, pp, tril, expand,
    xs, halo, act, scores, cum, rowt, total,
    msg, rcv, inco, inc, part, prec,
    local_sem, out_sem, wsend, wrecv, hsend, hrecv,
    msend, mrecv, isend, irecv, psend, precv, xsend, xrecv,
):
    core = lax.axis_index("section")
    me = lax.axis_index("block")
    other = 1 - core
    seqs, tokens, width = emb.shape
    half = wo.shape[1]
    bc = win.shape[2] - half
    nstate = bc // 2
    heads = msg.shape[2]
    head = half // heads
    inner = 2 * half
    rows = tokens // 2

    barrier = pltpu.get_barrier_semaphore()
    pl.semaphore_signal(barrier, inc=1, device_id={"section": other}, device_id_type=MESH)

    def greet(k, _):
        peer = lax.rem(me + k, blocks)
        pl.semaphore_signal(barrier, inc=1, device_id={"block": peer}, device_id_type=MESH)
        return 0

    lax.fori_loop(1, blocks, greet, 0)

    def half_at(which):
        return pl.ds(pl.multiple_of(which * half, half), half)

    loads = [
        pltpu.make_async_copy(emb, h.at[0], local_sem.at[0]),
        pltpu.make_async_copy(wide.at[0, :, half_at(core)], win.at[core, :, pl.ds(0, half)], local_sem.at[1]),
        pltpu.make_async_copy(wide.at[0, :, pl.ds(inner, bc)], win.at[core, :, pl.ds(half, bc)], local_sem.at[2]),
        pltpu.make_async_copy(proj.at[0, half_at(core), :], wo.at[core], local_sem.at[3]),
    ]
    for load in loads:
        load.start()

    pp[core, 0:4, :] = taps[0]
    pp[core, 4:5, :] = tbias[...]
    pp[core, 5:6, 0:width] = ngain[...]
    pp[core, 6:7, 0:inner] = igain[...]
    pp[core, 7:8, 0 : 2 * heads] = sbias[...]
    pp[core, 8:9, 0 : 2 * heads] = dlog[...]
    pp[core, 9:10, 0 : 2 * heads] = skip[...]
    rt[core] = rate[0]

    pl.semaphore_wait(barrier, blocks)

    def push(i, src, dst):
        return pltpu.make_async_remote_copy(
            src_ref=src, dst_ref=dst, send_sem=wsend.at[i], recv_sem=wrecv.at[i],
            device_id={"section": other}, device_id_type=MESH,
        )

    pushes = [
        push(0, wide.at[0, :, half_at(other)], win.at[core, :, pl.ds(0, half)]),
        push(1, wide.at[0, :, pl.ds(inner, bc)], win.at[core, :, pl.ds(half, bc)]),
        push(2, rt.at[core], rt.at[core]),
        push(3, pp.at[core], pp.at[core]),
        push(4, proj.at[0, half_at(other), :], wo.at[core]),
    ]
    for copy in pushes:
        copy.start()
    arrivals = [
        push(0, wide.at[0, :, half_at(core)], win.at[other, :, pl.ds(0, half)]),
        push(1, wide.at[0, :, pl.ds(inner, bc)], win.at[other, :, pl.ds(half, bc)]),
        push(2, rt.at[core], rt.at[other]),
        push(3, pp.at[core], pp.at[other]),
        push(4, proj.at[0, half_at(core), :], wo.at[other]),
    ]

    ri = lax.broadcasted_iota(jnp.int32, (tokens, tokens), 0)
    ci = lax.broadcasted_iota(jnp.int32, (tokens, tokens), 1)
    tril[...] = jnp.where(ri >= ci, 1.0, 0.0).astype(BF16)
    eh = lax.broadcasted_iota(jnp.int32, (heads, half), 0)
    ec = lax.broadcasted_iota(jnp.int32, (heads, half), 1)
    expand[...] = jnp.where((ec >= eh * head) & (ec < eh * head + head), 1.0, 0.0).astype(BF16)

    loads[0].wait()

    def mine(row):
        return jnp.where(core == 0, row[:, 0:heads], row[:, heads : 2 * heads])

    def halo_copy(l, s, peer):
        return pltpu.make_async_remote_copy(
            src_ref=xs.at[l, s, pl.ds(tokens, 8), :], dst_ref=halo.at[l, s],
            send_sem=hsend.at[l, s], recv_sem=hrecv.at[l, s],
            device_id={"block": peer}, device_id_type=MESH,
        )

    def state_copy(l, s, k):
        peer = lax.rem(me + k, blocks)
        return pltpu.make_async_remote_copy(
            src_ref=msg.at[l, s, peer], dst_ref=rcv.at[l, s, me],
            send_sem=msend.at[l, s, k], recv_sem=mrecv.at[l, s, me],
            device_id={"block": peer}, device_id_type=MESH,
        )

    def state_arrival(l, s, b):
        return pltpu.make_async_remote_copy(
            src_ref=msg.at[l, s, b], dst_ref=rcv.at[l, s, b],
            send_sem=msend.at[l, s, 0], recv_sem=mrecv.at[l, s, b],
            device_id={"block": b}, device_id_type=MESH,
        )

    def reply_copy(l, s, b):
        return pltpu.make_async_remote_copy(
            src_ref=inco.at[l, s, b], dst_ref=inc.at[l, s, me],
            send_sem=isend.at[l, s, b], recv_sem=irecv.at[l, s, me],
            device_id={"block": b}, device_id_type=MESH,
        )

    def reply_arrival(l, s, b):
        return pltpu.make_async_remote_copy(
            src_ref=inco.at[l, s, b], dst_ref=inc.at[l, s, b],
            send_sem=isend.at[l, s, b], recv_sem=irecv.at[l, s, b],
            device_id={"block": b}, device_id_type=MESH,
        )

    def rows_at(which):
        return pl.ds(pl.multiple_of(which * rows, rows), rows)

    def part_copy(l, s):
        return pltpu.make_async_remote_copy(
            src_ref=part.at[l, s, rows_at(other), :], dst_ref=prec.at[l, s],
            send_sem=psend.at[l, s], recv_sem=precv.at[l, s],
            device_id={"section": other}, device_id_type=MESH,
        )

    def hidden_copy(l, s, which):
        return pltpu.make_async_remote_copy(
            src_ref=h.at[l + 1, s, rows_at(which), :], dst_ref=h.at[l + 1, s, rows_at(which), :],
            send_sem=xsend.at[l, s], recv_sem=xrecv.at[l, s],
            device_id={"section": other}, device_id_type=MESH,
        )

    def front(l, s):
        if s == 0:
            @pl.when(l == core)
            def _():
                loads[1].wait()
                loads[2].wait()

            @pl.when(l != core)
            def _():
                for i in range(4):
                    arrivals[i].wait_recv()

        @pl.when(l > 0)
        def _():
            hidden_copy(l - 1, s, other).wait_recv()

        x = h[l, s].astype(F32)
        mean = jnp.mean(x * x, axis=-1, keepdims=True)
        normed = (x * lax.rsqrt(mean + EPS) * pp[l, 5:6, 0:width]).astype(BF16)
        for lo in range(0, half + bc, 256):
            xs[l, s, 8 : 8 + tokens, lo : lo + 256] = dot(normed, win[l, :, lo : lo + 256])

        @pl.when(me < blocks - 1)
        def _():
            halo_copy(l, s, me + 1).start()

        z = mine(dot(normed, rt[l])) + mine(pp[l, 7:8, 0 : 2 * heads])
        e = jnp.exp(-jnp.abs(z))
        small = e * (1.0 - e * (0.5 - e * (1.0 / 3.0 - e * 0.25)))
        step = jnp.maximum(z, 0.0) + jnp.where(e < 0.01, small, jnp.log(1.0 + e))
        ld = -step * (jnp.exp(mine(pp[l, 8:9, 0 : 2 * heads])) * LOG2E)
        hi = ld.astype(BF16)
        rest = ld - hi.astype(F32)
        mid, lo = split2(rest)
        low = tril[...]
        c = dot(low, hi) + dot(low, mid) + dot(low, lo)
        r = c - jnp.log(step) * LOG2E
        cum[s, :, 0:heads] = c
        padded = jnp.concatenate([r, jnp.zeros((tokens, 128 - heads), F32)], axis=1)
        rowt[s] = padded.T[0:heads]
        tail = jnp.exp2(c[tokens - 1 : tokens] - r)
        thi, tlo = split2(tail)
        total[s] = dot(thi, expand[...]) + dot(tlo, expand[...])

    def middle(l, s):
        @pl.when(me > 0)
        def _():
            halo_copy(l, s, me - 1).wait_recv()
            xs[l, s, 0:8, :] = halo[l, s]

        @pl.when(me == 0)
        def _():
            xs[l, s, 0:8, :] = jnp.zeros((8, half + bc), F32)

        ones = jnp.zeros((tokens, 128), F32)
        b_f32 = None
        for j in list(range(half // 128, (half + bc) // 128)) + list(range(half // 128)):
            lo = 128 * j
            if lo < half:
                col = pl.ds(pl.multiple_of(core * half + lo, 128), 128)
            else:
                col = pl.ds(inner + lo - half, 128)
            acc = pp[l, 4:5, col] + ones
            for k in range(4):
                acc = acc + xs[l, s, 5 + k : 5 + k + tokens, lo : lo + 128] * pp[l, k : k + 1, col]
            a = 0.5 * acc
            v = (a + a * jnp.tanh(a)).astype(BF16)
            act[s, :, lo : lo + 128] = v
            if lo == half:
                b_f32 = v.astype(F32)
        b = act[s, :, half : half + nstate]
        c = act[s, :, half + nstate : half + bc]
        scores[s] = dot_nt(c, b)
        bt = b_f32.T.astype(BF16)
        last = jnp.exp2(cum[s, tokens - 1 : tokens, 0:heads])
        for j in range(half // 128):
            lo = 128 * j
            weighted = (act[s, :, lo : lo + 128].astype(F32) * total[s, :, lo : lo + 128]).astype(BF16)
            state = dot(bt, weighted).T.astype(BF16)
            for q in range(2):
                hd = 2 * j + q
                msg[l, s, hd, 0:head, :] = state[head * q : head * (q + 1), :]
                d = jnp.broadcast_to(last[:, hd : hd + 1], (8, 128))
                dhi = d.astype(BF16).astype(F32)
                msg[l, s, hd, head : head + DECAY_ROWS, :] = jnp.concatenate([dhi, d - dhi], axis=0).astype(BF16)

        def send(k, _):
            state_copy(l, s, k).start()
            return 0

        lax.fori_loop(1, blocks, send, 0)

    def diagonal(l, s):
        hr = tokens // 2
        mask = lax.broadcasted_iota(jnp.int32, (hr, hr), 0) >= lax.broadcasted_iota(jnp.int32, (hr, hr), 1)
        lane = lax.broadcasted_iota(jnp.int32, (tokens, 128), 1) < head
        sk = mine(pp[l, 9:10, 0 : 2 * heads])
        for j in range(half // 128):
            lo = 128 * j
            vals = act[s, :, lo : lo + 128]
            zero = jnp.zeros_like(vals)
            gain = jnp.where(
                lane[0:1], jnp.broadcast_to(sk[:, 2 * j : 2 * j + 1], (1, 128)),
                jnp.broadcast_to(sk[:, 2 * j + 1 : 2 * j + 2], (1, 128)),
            )
            top = vals[0:hr].astype(F32) * gain
            bot = vals[hr:].astype(F32) * gain
            for q in range(2):
                hd = 2 * j + q
                v = jnp.where(lane, vals, zero) if q == 0 else jnp.where(lane, zero, vals)
                ct = jnp.broadcast_to(cum[s, 0:hr, hd : hd + 1], (hr, hr))
                cb = jnp.broadcast_to(cum[s, hr:tokens, hd : hd + 1], (hr, hr))
                r0 = rowt[s, hd : hd + 1, 0:hr]
                r1 = rowt[s, hd : hd + 1, hr:tokens]
                m00 = jnp.where(mask, jnp.exp2(ct - r0) * scores[s, 0:hr, 0:hr], 0.0).astype(BF16)
                m10 = (jnp.exp2(cb - r0) * scores[s, hr:tokens, 0:hr]).astype(BF16)
                m11 = jnp.where(mask, jnp.exp2(cb - r1) * scores[s, hr:tokens, hr:tokens], 0.0).astype(BF16)
                top = top + dot(m00, v[0:hr])
                bot = bot + dot(jnp.concatenate([m10, m11], axis=1), v)
            total[s, 0:hr, lo : lo + 128] = top
            total[s, hr:tokens, lo : lo + 128] = bot

    def scan(l, s):
        rcv[l, s, me] = msg[l, s, me]

        def step(b, state):
            @pl.when(b != me)
            def _():
                state_arrival(l, s, b).wait_recv()

            inco[l, s, b] = state.astype(BF16)

            @pl.when(b != me)
            def _():
                reply_copy(l, s, b).start()

            m = rcv[l, s, b].astype(F32)
            d = m[head : head + 8] + m[head + 8 : head + 16]
            return state * jnp.concatenate([d] * (head // 8), axis=0) + m[0:head]

        lax.fori_loop(0, blocks, step, jnp.zeros((head, nstate), F32))
        inc[l, s, me] = inco[l, s, me]

    def back(l, s):
        if s == 0:
            @pl.when(l == core)
            def _():
                loads[3].wait()

            @pl.when(l != core)
            def _():
                arrivals[4].wait_recv()

        def arrive(b, _):
            @pl.when(b != me)
            def _():
                reply_arrival(l, s, b).wait_recv()

            return 0

        lax.fori_loop(0, blocks, arrive, 0)
        c = act[s, :, half + nstate : half + bc]
        ehi, elo = split2(jnp.exp2(cum[s, :, 0:heads]))
        sq = jnp.zeros((tokens, 1), F32)
        ys = []
        per = 256 // head
        for j in range(half // 256):
            lo = 256 * j
            incoming = inc[l, s, per * j : per * (j + 1)].reshape(256, nstate)
            e = dot(ehi, expand[:, lo : lo + 256]) + dot(elo, expand[:, lo : lo + 256])
            t = total[s, :, lo : lo + 256] + dot_nt(c, incoming) * e
            sq = sq + jnp.sum(t * t, axis=-1, keepdims=True)
            gain = pp[l, 6:7, pl.ds(pl.multiple_of(core * half + lo, 256), 256)]
            ys.append((t * gain).astype(BF16))
        y = jnp.concatenate(ys, axis=1)
        for lo in range(0, width, 256):
            part[l, s, :, lo : lo + 256] = dot(y, wo[l, :, lo : lo + 256])
        part[l, s, :, width : width + 128] = jnp.broadcast_to(sq, (tokens, 128))
        part_copy(l, s).start()

    def finish(l, s):
        part_copy(l, s).wait_recv()
        at = rows_at(core)
        sq = part[l, s, at, width : width + 128] + prec[l, s, :, width : width + 128]
        scale = lax.rsqrt(sq * (1.0 / inner) + EPS)
        for lo in range(0, width, 128):
            y = part[l, s, at, lo : lo + 128] + prec[l, s, :, lo : lo + 128]
            new = h[l, s, at, lo : lo + 128].astype(F32) + y * scale
            h[l + 1, s, at, lo : lo + 128] = new.astype(BF16)
        hidden_copy(l, s, core).start()

    def layer(l, _):
        front(l, 0)
        front(l, 1)
        middle(l, 0)
        middle(l, 1)
        diagonal(l, 0)
        scan(l, 0)
        diagonal(l, 1)
        scan(l, 1)
        back(l, 0)
        back(l, 1)
        finish(l, 0)
        finish(l, 1)
        return 0

    lax.fori_loop(0, 2, layer, 0)

    for s in range(seqs):
        hidden_copy(1, s, other).wait_recv()
    result = pltpu.make_async_copy(h.at[core + 1], out.at[0], out_sem)
    result.start()
    for copy in pushes:
        copy.wait_send()

    def drain(l, _):
        for s in range(seqs):
            @pl.when(me < blocks - 1)
            def _():
                halo_copy(l, s, me + 1).wait_send()

            part_copy(l, s).wait_send()
            hidden_copy(l, s, core).wait_send()

            def one(k, _):
                state_copy(l, s, k).wait_send()
                reply_copy(l, s, lax.rem(me + k, blocks)).wait_send()
                return 0

            lax.fori_loop(1, blocks, one, 0)
        return 0

    lax.fori_loop(0, 2, drain, 0)
    result.wait()


def shards(emb, wide, rate, taps, tbias, sbias, dlog, skip, ngain, igain, proj):
    blocks = lax.axis_size("block")
    seqs, tokens, width = emb.shape
    xbc = wide.shape[2]
    inner = proj.shape[1]
    half = inner // 2
    bc = xbc - inner
    heads = sbias.shape[1] // 2
    head = half // heads
    nstate = bc // 2
    assert heads == blocks and lax.axis_size("section") == 2
    vmem = pl.BlockSpec(memory_space=pltpu.VMEM)
    hbm = pl.BlockSpec(memory_space=pl.ANY)
    V, dma = pltpu.VMEM, pltpu.SemaphoreType.DMA
    return pl.pallas_call(
        functools.partial(kernel, blocks),
        out_shape=jax.ShapeDtypeStruct((1, seqs, tokens, width), BF16),
        in_specs=[hbm, hbm] + [vmem] * 8 + [hbm],
        out_specs=hbm,
        scratch_shapes=[
            V((3, seqs, tokens, width), BF16),
            V((2, width, half + bc), BF16),
            V((2, half, width), BF16),
            V((2, width, 2 * heads), BF16),
            V((2, 16, xbc), F32),
            V((tokens, tokens), BF16),
            V((heads, half), BF16),
            V((2, seqs, tokens + 8, half + bc), F32),
            V((2, seqs, 8, half + bc), F32),
            V((seqs, tokens, half + bc), BF16),
            V((seqs, tokens, tokens), F32),
            V((seqs, tokens, 128), F32),
            V((seqs, heads, tokens), F32),
            V((seqs, tokens, half), F32),
            V((2, seqs, blocks, head + DECAY_ROWS, nstate), BF16),
            V((2, seqs, blocks, head + DECAY_ROWS, nstate), BF16),
            V((2, seqs, blocks, head, nstate), BF16),
            V((2, seqs, blocks, head, nstate), BF16),
            V((2, seqs, tokens, width + 128), F32),
            V((2, seqs, tokens // 2, width + 128), F32),
            dma((4,)), dma(()), dma((5,)), dma((5,)),
            dma((2, seqs)), dma((2, seqs)),
            dma((2, seqs, blocks)), dma((2, seqs, blocks)),
            dma((2, seqs, blocks)), dma((2, seqs, blocks)),
            dma((2, seqs)), dma((2, seqs)), dma((2, seqs)), dma((2, seqs)),
        ],
        compiler_params=pltpu.CompilerParams(
            collective_id=0, has_side_effects=True, vmem_limit_bytes=52 * 1024 * 1024
        ),
    )(emb, wide, rate, taps, tbias, sbias, dlog, skip, ngain, igain, proj)


def solution(mesh):
    placed = (
        P("dp", "block", None),
        P("section", None, None),
        P("section", None, None),
        P("section", None, None),
        P("section", None),
        P("section", None),
        P("section", None),
        P("section", None),
        P("section", None),
        P("section", None),
        P("section", None, None),
    )
    return jax.shard_map(
        shards,
        mesh=mesh,
        in_specs=placed,
        out_specs=P("section", "dp", "block", None),
        check_vma=False,
    )
```

```python
import functools

import jax
import jax.numpy as jnp
from jax import lax
from jax.experimental import pallas as pl
from jax.experimental.pallas import tpu as pltpu
from jax.sharding import PartitionSpec as P

MESH = pl.DeviceIdType.MESH
F32, BF16 = jnp.float32, jnp.bfloat16
LOG2E = 1.4426950408889634
EPS = 1e-05
DECAY_ROWS = 16


def split2(x):
    hi = x.astype(BF16)
    return hi, (x - hi.astype(F32)).astype(BF16)


def dot(a, b):
    return jnp.dot(a, b, preferred_element_type=F32)


def dot_nt(a, b):
    return lax.dot_general(a, b, (((1,), (1,)), ((), ())), preferred_element_type=F32)


def kernel(
    blocks,
    emb, wide, rate, taps, tbias, sbias, dlog, skip, ngain, igain, proj,
    out,
    h, edge, nx, win, wo, rt, tp, tb, sb, dl, sg, ng, ig, triu, expand, colc,
    xs, halo, act, scores, cum, cols16, rowt, dk, total,
    msg, rcv, inco, inc, part, prec,
    local_sem, wsend, wrecv, esend, erecv, hsend, hrecv,
    msend, mrecv, isend, irecv, psend, precv,
):
    core = lax.axis_index("section")
    me = lax.axis_index("block")
    other = 1 - core
    seqs, tokens, width = emb.shape
    half = wo.shape[1]
    bc = win.shape[2] - half
    nstate = bc // 2
    heads = msg.shape[2]
    head = half // heads
    inner = 2 * half
    edge_rows = edge.shape[1]
    cols = 256
    chunks = (half + bc) // cols
    pieces = ((0, width // 2), (width // 2, width + 128))

    barrier = pltpu.get_barrier_semaphore()
    pl.semaphore_signal(barrier, inc=1, device_id={"section": other}, device_id_type=MESH)

    def greet(k, _):
        peer = lax.rem(me + k, blocks)
        pl.semaphore_signal(barrier, inc=1, device_id={"block": peer}, device_id_type=MESH)
        return 0

    lax.fori_loop(1, blocks, greet, 0)

    def moves(which, layer):
        found = []
        for j in range(chunks):
            at = which * half + cols * j if cols * j < half else inner + cols * j - half
            found.append((wide.at[0, :, pl.ds(pl.multiple_of(at, cols), cols)], win.at[layer, :, pl.ds(cols * j, cols)]))
        found += [(rate.at[0], rt.at[layer]), (taps.at[0], tp.at[layer])]
        found += [(a, b.at[layer]) for a, b in ((tbias, tb), (sbias, sb), (dlog, dl), (skip, sg), (ngain, ng), (igain, ig))]
        found.append((proj.at[0, pl.ds(pl.multiple_of(which * half, half), half), :], wo.at[layer]))
        return found

    local = [pltpu.make_async_copy(a, b, local_sem.at[i]) for i, (a, b) in enumerate(moves(core, core))]
    count = len(local)
    embed = pltpu.make_async_copy(emb, h.at[0], local_sem.at[count])
    embed.start()
    for copy in local[chunks:-1] + local[:chunks] + local[-1:]:
        copy.start()

    def remote(i, move):
        return pltpu.make_async_remote_copy(
            src_ref=move[0], dst_ref=move[1], send_sem=wsend.at[i], recv_sem=wrecv.at[i],
            device_id={"section": other}, device_id_type=MESH,
        )

    pushes = [remote(i, m) for i, m in enumerate(moves(other, core))]
    arrivals = [remote(i, m) for i, m in enumerate(moves(core, other))]

    def edge_copy(peer):
        return pltpu.make_async_remote_copy(
            src_ref=emb.at[:, pl.ds(tokens - edge_rows, edge_rows), :], dst_ref=edge,
            send_sem=esend, recv_sem=erecv, device_id={"block": peer}, device_id_type=MESH,
        )

    pl.semaphore_wait(barrier, blocks)
    for copy in pushes[chunks:-1] + pushes[:chunks]:
        copy.start()

    @pl.when(me < blocks - 1)
    def _():
        edge_copy(me + 1).start()

    def ready(l, which):
        @pl.when(core == l)
        def _():
            for i in which:
                local[i].wait()

        @pl.when(core != l)
        def _():
            for i in which:
                arrivals[i].wait_recv()

    ri = lax.broadcasted_iota(jnp.int32, (tokens, tokens), 0)
    ci = lax.broadcasted_iota(jnp.int32, (tokens, tokens), 1)
    triu[...] = jnp.where(ri <= ci, 1.0, 0.0).astype(BF16)
    eh = lax.broadcasted_iota(jnp.int32, (heads, half), 0)
    ec = lax.broadcasted_iota(jnp.int32, (heads, half), 1)
    spread = jnp.where((ec >= eh * head) & (ec < eh * head + head), 1.0, 0.0).astype(BF16)
    expand[...] = jnp.zeros_like(expand)
    for i, lo in ((1, 0), (2, 0), (3, half), (4, half)):
        expand[heads * i : heads * (i + 1), lo : lo + half] = spread

    def mine(row):
        return jnp.where(core == 0, row[:, 0:heads], row[:, heads : 2 * heads])

    def halo_copy(s, peer):
        return pltpu.make_async_remote_copy(
            src_ref=xs.at[1, s, pl.ds(tokens, 8), :], dst_ref=halo.at[s],
            send_sem=hsend.at[s], recv_sem=hrecv.at[s],
            device_id={"block": peer}, device_id_type=MESH,
        )

    def state_copy(l, s, k):
        peer = lax.rem(me + k, blocks)
        return pltpu.make_async_remote_copy(
            src_ref=msg.at[l, s, peer], dst_ref=rcv.at[l, s, me],
            send_sem=msend.at[l, s, k], recv_sem=mrecv.at[l, s, me],
            device_id={"block": peer}, device_id_type=MESH,
        )

    def state_arrival(l, s, b):
        return pltpu.make_async_remote_copy(
            src_ref=msg.at[l, s, b], dst_ref=rcv.at[l, s, b],
            send_sem=msend.at[l, s, 0], recv_sem=mrecv.at[l, s, b],
            device_id={"block": b}, device_id_type=MESH,
        )

    def reply_copy(l, s, b):
        return pltpu.make_async_remote_copy(
            src_ref=inco.at[l, s, b], dst_ref=inc.at[l, s, me],
            send_sem=isend.at[l, s, b], recv_sem=irecv.at[l, s, me],
            device_id={"block": b}, device_id_type=MESH,
        )

    def reply_arrival(l, s, b):
        return pltpu.make_async_remote_copy(
            src_ref=inco.at[l, s, b], dst_ref=inc.at[l, s, b],
            send_sem=isend.at[l, s, b], recv_sem=irecv.at[l, s, b],
            device_id={"block": b}, device_id_type=MESH,
        )

    def part_copy(l, s, i):
        at = pl.ds(pieces[i][0], pieces[i][1] - pieces[i][0])
        return pltpu.make_async_remote_copy(
            src_ref=part.at[l, s, :, at], dst_ref=prec.at[l, s, :, at],
            send_sem=psend.at[l, s, i], recv_sem=precv.at[l, s, i],
            device_id={"section": other}, device_id_type=MESH,
        )

    def normalize(l, x):
        x = x.astype(F32)
        mean = jnp.mean(x * x, axis=-1, keepdims=True)
        return (x * lax.rsqrt(mean + EPS) * ng[l]).astype(BF16)

    def columns(l):
        ready(l, range(chunks, count - 1))
        for i, row in ((0, mine(sb[l])), (1, jnp.exp(mine(dl[l])) * LOG2E)):
            wide_row = jnp.concatenate([row, jnp.zeros((1, 128 - heads), F32)], axis=1)
            colc[l, i] = jnp.broadcast_to(wide_row, (128, 128)).T[0:heads]

    def rates(l, s, normed):
        both = dot_nt(rt[l], normed)
        z = jnp.where(core == 0, both[0:heads], both[heads : 2 * heads])
        z = z + jnp.concatenate([colc[l, 0]] * (tokens // 128), axis=1)
        e = jnp.exp(-jnp.abs(z))
        small = e * (1.0 - e * (0.5 - e * (1.0 / 3.0 - e * 0.25)))
        step = jnp.maximum(z, 0.0) + jnp.where(e < 0.01, small, jnp.log(1.0 + e))
        ld = -step * jnp.concatenate([colc[l, 1]] * (tokens // 128), axis=1)
        hi = ld.astype(BF16)
        mid, lo = split2(ld - hi.astype(F32))
        c3 = dot(jnp.concatenate([hi, mid, lo], axis=0), triu[...])
        c = c3[0:heads] + c3[heads : 2 * heads] + c3[2 * heads : 3 * heads]
        r = c - jnp.log(step) * LOG2E
        rowt[s] = r
        last = jnp.broadcast_to(c[:, tokens - 1 : tokens], (heads, tokens))
        tail = jnp.exp2(last - r)
        thi = tail.astype(BF16).astype(F32)
        grown = jnp.exp2(c)
        ghi = grown.astype(BF16).astype(F32)
        stack = [c, thi, tail - thi, ghi, grown - ghi, jnp.zeros((128 - 5 * heads, tokens), F32)]
        col = jnp.concatenate(stack, axis=0).T
        cum[s] = col
        narrow = col.astype(BF16)
        cols16[s] = narrow
        total[s] = dot(narrow, expand[:, 0:half])
        d = jnp.exp2(last[:, 0:128])
        dhi = d.astype(BF16).astype(F32)
        dk[s, 0:heads] = dhi
        dk[s, heads : 2 * heads] = d - dhi

    def front_both():
        embed.wait()
        columns(0)
        span = edge_rows + tokens
        for s in range(seqs):
            normed = normalize(0, h[0, s])
            nx[span * s + edge_rows : span * (s + 1)] = normed
            rates(0, s, normed)

        @pl.when(me > 0)
        def _():
            edge_copy(me).wait_recv()

        @pl.when(me == 0)
        def _():
            edge[...] = jnp.zeros_like(edge)

        for s in range(seqs):
            nx[span * s : span * s + edge_rows] = normalize(0, edge[s])
        for j in range(chunks):
            ready(0, [j])
            made = dot(nx[...], win[0, :, cols * j : cols * (j + 1)])
            for s in range(seqs):
                xs[0, s, :, cols * j : cols * (j + 1)] = made[span * (s + 1) - tokens - 8 : span * (s + 1)]

    def front(s):
        normed = normalize(1, h[1, s])
        for lo in range(0, half + bc, cols):
            xs[1, s, 8 : 8 + tokens, lo : lo + cols] = dot(normed, win[1, :, lo : lo + cols])

        @pl.when(me < blocks - 1)
        def _():
            halo_copy(s, me + 1).start()

        rates(1, s, normed)

    def middle(l, s):
        if l == 1:
            @pl.when(me > 0)
            def _():
                halo_copy(s, me).wait_recv()
                xs[1, s, 0:8, :] = halo[s]

            @pl.when(me == 0)
            def _():
                xs[1, s, 0:8, :] = jnp.zeros((8, half + bc), F32)

        b_f32 = None
        for j in list(range(half // 128, (half + bc) // 128)) + list(range(half // 128)):
            lo = 128 * j
            if lo < half:
                col = pl.ds(pl.multiple_of(core * half + lo, 128), 128)
            else:
                col = pl.ds(inner + lo - half, 128)
            acc = tb[l, :, col] + xs[l, s, 8 : 8 + tokens, lo : lo + 128] * tp[l, 3:4, col]
            for k in range(3):
                acc = acc + xs[l, s, 5 + k : 5 + k + tokens, lo : lo + 128] * tp[l, k : k + 1, col]
            a = 0.5 * acc
            v = (a + a * jnp.tanh(a)).astype(BF16)
            act[s, :, lo : lo + 128] = v
            if lo == half:
                b_f32 = v.astype(F32)
        bt = b_f32.T.astype(BF16)
        for j in range(half // 128):
            lo = 128 * j
            weighted = (act[s, :, lo : lo + 128].astype(F32) * total[s, :, lo : lo + 128]).astype(BF16)
            state = dot(bt, weighted).T.astype(BF16)
            for q in range(2):
                hd = 2 * j + q
                msg[l, s, hd, 0:head, :] = state[head * q : head * (q + 1), :]
                both = [jnp.broadcast_to(dk[s, i : i + 1, :], (8, 128)) for i in (hd, heads + hd)]
                msg[l, s, hd, head : head + DECAY_ROWS, :] = jnp.concatenate(both, axis=0).astype(BF16)

        def send(k, _):
            state_copy(l, s, k).start()
            return 0

        lax.fori_loop(1, blocks, send, 0)

    def diagonal(l, s):
        hr = tokens // 2
        b = act[s, :, half : half + nstate]
        c = act[s, :, half + nstate : half + bc]
        scores[...] = dot_nt(c, b)
        mask = lax.broadcasted_iota(jnp.int32, (hr, hr), 0) >= lax.broadcasted_iota(jnp.int32, (hr, hr), 1)
        lane = lax.broadcasted_iota(jnp.int32, (tokens, 128), 1) < head
        sk = mine(sg[l])
        for j in range(half // 128):
            lo = 128 * j
            vals = act[s, :, lo : lo + 128]
            zero = jnp.zeros_like(vals)
            gain = jnp.where(
                lane[0:1], jnp.broadcast_to(sk[:, 2 * j : 2 * j + 1], (1, 128)),
                jnp.broadcast_to(sk[:, 2 * j + 1 : 2 * j + 2], (1, 128)),
            )
            top = vals[0:hr].astype(F32) * gain
            bot = vals[hr:].astype(F32) * gain
            for q in range(2):
                hd = 2 * j + q
                v = jnp.where(lane, vals, zero) if q == 0 else jnp.where(lane, zero, vals)
                ct = jnp.broadcast_to(cum[s, 0:hr, hd : hd + 1], (hr, hr))
                cb = jnp.broadcast_to(cum[s, hr:tokens, hd : hd + 1], (hr, hr))
                r0 = rowt[s, hd : hd + 1, 0:hr]
                r1 = rowt[s, hd : hd + 1, hr:tokens]
                m00 = jnp.where(mask, jnp.exp2(ct - r0) * scores[0:hr, 0:hr], 0.0).astype(BF16)
                m10 = (jnp.exp2(cb - r0) * scores[hr:tokens, 0:hr]).astype(BF16)
                m11 = jnp.where(mask, jnp.exp2(cb - r1) * scores[hr:tokens, hr:tokens], 0.0).astype(BF16)
                top = top + dot(m00, v[0:hr])
                bot = bot + dot(jnp.concatenate([m10, m11], axis=1), v)
            total[s, 0:hr, lo : lo + 128] = top
            total[s, hr:tokens, lo : lo + 128] = bot

    def scan(l, s):
        rcv[l, s, me] = msg[l, s, me]

        def step(b, state):
            @pl.when(b != me)
            def _():
                state_arrival(l, s, b).wait_recv()

            inco[l, s, b] = state.astype(BF16)

            @pl.when(b != me)
            def _():
                reply_copy(l, s, b).start()

            m = rcv[l, s, b].astype(F32)
            d = m[head : head + 8] + m[head + 8 : head + 16]
            return state * jnp.concatenate([d] * (head // 8), axis=0) + m[0:head]

        lax.fori_loop(0, blocks, step, jnp.zeros((head, nstate), F32))
        inc[l, s, me] = inco[l, s, me]

    def back(l, s):
        if s == 0:
            ready(l, [count - 1])

        def arrive(b, _):
            @pl.when(b != me)
            def _():
                reply_arrival(l, s, b).wait_recv()

            return 0

        c = act[s, :, half + nstate : half + bc]
        grown = cols16[s]
        sq = jnp.zeros((tokens, 1), F32)
        ys = []
        per = 256 // head
        for j in range(half // 256):
            lo = 256 * j
            lax.fori_loop(per * j, per * (j + 1), arrive, 0)
            incoming = inc[l, s, per * j : per * (j + 1)].reshape(256, nstate)
            e = dot(grown, expand[:, half + lo : half + lo + 256])
            t = total[s, :, lo : lo + 256] + dot_nt(c, incoming) * e
            sq = sq + jnp.sum(t * t, axis=-1, keepdims=True)
            gain = ig[l, :, pl.ds(pl.multiple_of(core * half + lo, 256), 256)]
            ys.append((t * gain).astype(BF16))
        y = jnp.concatenate(ys, axis=1)
        shi = sq.astype(BF16).astype(F32)
        first = lax.broadcasted_iota(jnp.int32, (tokens, 128), 1) < 64
        part[l, s, :, width : width + 128] = jnp.where(first, shi, sq - shi).astype(BF16)
        for i in range(2):
            for lo in range(width // 2 * i, width // 2 * (i + 1), cols):
                part[l, s, :, lo : lo + cols] = dot(y, wo[l, :, lo : lo + cols]).astype(BF16)
            if l == 0:
                part_copy(l, s, i).start()
            else:
                pl.when(core == 0)(part_copy(l, s, i).start)

    def finish(l, s, store):
        for i in range(2):
            part_copy(l, s, i).wait_recv()
        sq = 0.0
        for lo in (width, width + 64):
            sq = sq + part[l, s, :, lo : lo + 1].astype(F32) + prec[l, s, :, lo : lo + 1].astype(F32)
        scale = jnp.broadcast_to(lax.rsqrt(sq * (1.0 / inner) + EPS), (tokens, 128))
        for lo in range(0, width, 128):
            y = part[l, s, :, lo : lo + 128].astype(F32) + prec[l, s, :, lo : lo + 128].astype(F32)
            new = h[l, s, :, lo : lo + 128].astype(F32) + y * scale
            store(lo, new.astype(BF16))

    def hidden_store(s):
        def store(lo, new):
            h[1, s, :, lo : lo + 128] = new

        return store

    def result_store(s):
        def store(lo, new):
            out[0, s, :, lo : lo + 128] = new

        return store

    def exchange(l):
        middle(l, 0)
        middle(l, 1)
        if l == 0:
            pushes[-1].start()
            columns(1)
        else:
            @pl.when(core == 0)
            def _():
                out[0] = h[1]
        diagonal(l, 0)
        scan(l, 0)
        diagonal(l, 1)
        scan(l, 1)
        back(l, 0)
        back(l, 1)

    front_both()
    exchange(0)
    ready(1, range(chunks))
    for s in range(seqs):
        finish(0, s, hidden_store(s))
        front(s)
    exchange(1)
    for s in range(seqs):
        pl.when(core == 1)(functools.partial(finish, 1, s, result_store(s)))

    for copy in pushes:
        copy.wait_send()

    @pl.when(me < blocks - 1)
    def _():
        edge_copy(me + 1).wait_send()
        for s in range(seqs):
            halo_copy(s, me + 1).wait_send()

    for s in range(seqs):
        for i in range(2):
            part_copy(0, s, i).wait_send()
            pl.when(core == 0)(part_copy(1, s, i).wait_send)

    def drain(k, _):
        for l in range(2):
            for s in range(seqs):
                state_copy(l, s, k).wait_send()
                reply_copy(l, s, lax.rem(me + k, blocks)).wait_send()
        return 0

    lax.fori_loop(1, blocks, drain, 0)


def shards(emb, wide, rate, taps, tbias, sbias, dlog, skip, ngain, igain, proj):
    blocks = lax.axis_size("block")
    seqs, tokens, width = emb.shape
    xbc = wide.shape[2]
    inner = proj.shape[1]
    half = inner // 2
    bc = xbc - inner
    heads = sbias.shape[1] // 2
    head = half // heads
    nstate = bc // 2
    assert heads == blocks and lax.axis_size("section") == 2
    hbm = pl.BlockSpec(memory_space=pltpu.HBM)
    V, dma = pltpu.VMEM, pltpu.SemaphoreType.DMA
    moved = (half + bc) // 256 + 9
    return pl.pallas_call(
        functools.partial(kernel, blocks),
        out_shape=jax.ShapeDtypeStruct((1, seqs, tokens, width), BF16),
        in_specs=[hbm] * 11,
        out_specs=pl.BlockSpec(memory_space=pltpu.VMEM),
        scratch_shapes=[
            V((2, seqs, tokens, width), BF16),
            V((seqs, 16, width), BF16),
            V((seqs * (tokens + 16), width), BF16),
            V((2, width, half + bc), BF16),
            V((2, half, width), BF16),
            V((2, 2 * heads, width), BF16),
            V((2, 4, xbc), F32),
            V((2, 1, xbc), F32),
            V((2, 1, 2 * heads), F32),
            V((2, 1, 2 * heads), F32),
            V((2, 1, 2 * heads), F32),
            V((2, 1, width), F32),
            V((2, 1, inner), F32),
            V((tokens, tokens), BF16),
            V((128, 2 * half), BF16),
            V((2, 2, heads, 128), F32),
            V((2, seqs, tokens + 8, half + bc), F32),
            V((seqs, 8, half + bc), F32),
            V((seqs, tokens, half + bc), BF16),
            V((tokens, tokens), F32),
            V((seqs, tokens, 128), F32),
            V((seqs, tokens, 128), BF16),
            V((seqs, heads, tokens), F32),
            V((seqs, 2 * heads, 128), F32),
            V((seqs, tokens, half), F32),
            V((2, seqs, blocks, head + DECAY_ROWS, nstate), BF16),
            V((2, seqs, blocks, head + DECAY_ROWS, nstate), BF16),
            V((2, seqs, blocks, head, nstate), BF16),
            V((2, seqs, blocks, head, nstate), BF16),
            V((2, seqs, tokens, width + 128), BF16),
            V((2, seqs, tokens, width + 128), BF16),
            dma((moved + 1,)), dma((moved,)), dma((moved,)), dma(()), dma(()),
            dma((seqs,)), dma((seqs,)),
            dma((2, seqs, blocks)), dma((2, seqs, blocks)),
            dma((2, seqs, blocks)), dma((2, seqs, blocks)),
            dma((2, seqs, 2)), dma((2, seqs, 2)),
        ],
        compiler_params=pltpu.CompilerParams(
            collective_id=0, has_side_effects=True, vmem_limit_bytes=63 * 1024 * 1024
        ),
    )(emb, wide, jnp.swapaxes(rate, 1, 2), taps, tbias, sbias, dlog, skip, ngain, igain, proj)


def solution(mesh):
    placed = (
        P("dp", "block", None),
        P("section", None, None),
        P("section", None, None),
        P("section", None, None),
        P("section", None),
        P("section", None),
        P("section", None),
        P("section", None),
        P("section", None),
        P("section", None),
        P("section", None, None),
    )
    return jax.shard_map(
        shards,
        mesh=mesh,
        in_specs=placed,
        out_specs=P("section", "dp", "block", None),
        check_vma=False,
    )
```

```python
import functools

import jax
import jax.numpy as jnp
from jax import lax
from jax.experimental import pallas as pl
from jax.experimental.pallas import tpu as pltpu
from jax.sharding import PartitionSpec as P

MESH = pl.DeviceIdType.MESH
F32, BF16 = jnp.float32, jnp.bfloat16
LOG2E = 1.4426950408889634
EPS = 1e-05
DECAY_ROWS = 16


def split2(x):
    hi = x.astype(BF16)
    return hi, (x - hi.astype(F32)).astype(BF16)


def dot(a, b):
    return jnp.dot(a, b, preferred_element_type=F32)


def dot_nt(a, b):
    return lax.dot_general(a, b, (((1,), (1,)), ((), ())), preferred_element_type=F32)


def kernel(
    blocks,
    emb, wide, rate, taps, tbias, sbias, dlog, skip, ngain, igain, proj,
    out,
    h, edge, nx, win, wo, rt, rk, tp, tb, sb, dl, sg, ng, ig, triu, expand, colc,
    xs, halo, act, scores, cum, cols16, rowt, dk, total,
    msg, rcv, inco, inc, part, prec,
    local_sem, wsend, wrecv, esend, erecv, hsend, hrecv,
    msend, mrecv, isend, irecv, psend, precv,
):
    core = lax.axis_index("section")
    me = lax.axis_index("block")
    other = 1 - core
    seqs, tokens, width = emb.shape
    half = wo.shape[1]
    bc = win.shape[2] - half
    nstate = bc // 2
    heads = msg.shape[2]
    head = half // heads
    inner = 2 * half
    edge_rows = edge.shape[1]
    cols = 256
    chunks = (half + bc) // cols
    pieces = [(0 if lo == 0 else lo + 128, lo + 128 + cols) for lo in range(0, width, cols)]

    barrier = pltpu.get_barrier_semaphore()
    pl.semaphore_signal(barrier, inc=1, device_id={"section": other}, device_id_type=MESH)

    def greet(k, _):
        peer = lax.rem(me + k, blocks)
        pl.semaphore_signal(barrier, inc=1, device_id={"block": peer}, device_id_type=MESH)
        return 0

    lax.fori_loop(1, blocks, greet, 0)

    def moves(which, layer):
        found = []
        for j in range(chunks):
            at = which * half + cols * j if cols * j < half else inner + cols * j - half
            found.append((wide.at[0, :, pl.ds(pl.multiple_of(at, cols), cols)], win.at[layer, :, pl.ds(cols * j, cols)]))
        found += [(rate.at[0], rt.at[layer]), (taps.at[0], tp.at[layer])]
        found += [(a, b.at[layer]) for a, b in ((tbias, tb), (sbias, sb), (dlog, dl), (skip, sg), (ngain, ng), (igain, ig))]
        found.append((proj.at[0, pl.ds(pl.multiple_of(which * half, half), half), :], wo.at[layer]))
        return found

    local = [pltpu.make_async_copy(a, b, local_sem.at[i]) for i, (a, b) in enumerate(moves(core, core))]
    count = len(local)
    embed = pltpu.make_async_copy(emb, h.at[0], local_sem.at[count])
    embed.start()
    for copy in local[chunks:-1] + local[:chunks] + local[-1:]:
        copy.start()

    def remote(i, move):
        return pltpu.make_async_remote_copy(
            src_ref=move[0], dst_ref=move[1], send_sem=wsend.at[i], recv_sem=wrecv.at[i],
            device_id={"section": other}, device_id_type=MESH,
        )

    pushes = [remote(i, m) for i, m in enumerate(moves(other, core))]
    arrivals = [remote(i, m) for i, m in enumerate(moves(core, other))]

    def edge_copy(peer):
        return pltpu.make_async_remote_copy(
            src_ref=emb.at[:, pl.ds(tokens - edge_rows, edge_rows), :], dst_ref=edge,
            send_sem=esend, recv_sem=erecv, device_id={"block": peer}, device_id_type=MESH,
        )

    pl.semaphore_wait(barrier, blocks)
    for copy in pushes[chunks:-1] + pushes[:chunks]:
        copy.start()

    @pl.when(me < blocks - 1)
    def _():
        edge_copy(me + 1).start()

    def ready(l, which):
        @pl.when(core == l)
        def _():
            for i in which:
                local[i].wait()

        @pl.when(core != l)
        def _():
            for i in which:
                arrivals[i].wait_recv()

    ri = lax.broadcasted_iota(jnp.int32, (tokens, tokens), 0)
    ci = lax.broadcasted_iota(jnp.int32, (tokens, tokens), 1)
    triu[...] = jnp.where(ri <= ci, 1.0, 0.0).astype(BF16)
    eh = lax.broadcasted_iota(jnp.int32, (heads, half), 0)
    ec = lax.broadcasted_iota(jnp.int32, (heads, half), 1)
    spread = jnp.where((ec >= eh * head) & (ec < eh * head + head), 1.0, 0.0).astype(BF16)
    expand[...] = jnp.zeros_like(expand)
    for i, lo in ((1, 0), (2, 0), (3, half), (4, half)):
        expand[heads * i : heads * (i + 1), lo : lo + half] = spread

    def mine(row):
        return jnp.where(core == 0, row[:, 0:heads], row[:, heads : 2 * heads])

    def halo_copy(s, peer):
        return pltpu.make_async_remote_copy(
            src_ref=xs.at[1, s, pl.ds(tokens, 8), :], dst_ref=halo.at[s],
            send_sem=hsend.at[s], recv_sem=hrecv.at[s],
            device_id={"block": peer}, device_id_type=MESH,
        )

    def state_copy(l, s, b):
        return pltpu.make_async_remote_copy(
            src_ref=msg.at[l, s, b], dst_ref=rcv.at[l, s, me],
            send_sem=msend.at[l, s, b], recv_sem=mrecv.at[l, s, me],
            device_id={"block": b}, device_id_type=MESH,
        )

    def state_arrival(l, s, b):
        return pltpu.make_async_remote_copy(
            src_ref=msg.at[l, s, b], dst_ref=rcv.at[l, s, b],
            send_sem=msend.at[l, s, b], recv_sem=mrecv.at[l, s, b],
            device_id={"block": b}, device_id_type=MESH,
        )

    def reply_copy(l, s, b):
        return pltpu.make_async_remote_copy(
            src_ref=inco.at[l, s, b], dst_ref=inc.at[l, s, me],
            send_sem=isend.at[l, s, b], recv_sem=irecv.at[l, s, me],
            device_id={"block": b}, device_id_type=MESH,
        )

    def reply_arrival(l, s, b):
        return pltpu.make_async_remote_copy(
            src_ref=inco.at[l, s, b], dst_ref=inc.at[l, s, b],
            send_sem=isend.at[l, s, b], recv_sem=irecv.at[l, s, b],
            device_id={"block": b}, device_id_type=MESH,
        )

    def part_copy(l, s, i):
        at = pl.ds(pieces[i][0], pieces[i][1] - pieces[i][0])
        return pltpu.make_async_remote_copy(
            src_ref=part.at[l, s, :, at], dst_ref=prec.at[l, s, :, at],
            send_sem=psend.at[l, s, i], recv_sem=precv.at[l, s, i],
            device_id={"section": other}, device_id_type=MESH,
        )

    def normalize(l, x):
        x = x.astype(F32)
        mean = jnp.mean(x * x, axis=-1, keepdims=True)
        return (x * lax.rsqrt(mean + EPS) * ng[l]).astype(BF16)

    def columns(l):
        ready(l, range(chunks, count - 1))
        for i, row in ((0, mine(sb[l])), (1, jnp.exp(mine(dl[l])) * LOG2E)):
            wide_row = jnp.concatenate([row, jnp.zeros((1, 128 - heads), F32)], axis=1)
            colc[l, i] = jnp.broadcast_to(wide_row, (128, 128)).T[0:heads]
        tall = jnp.concatenate([rt[l].astype(F32), jnp.zeros((128 - 2 * heads, width), F32)], axis=0)
        rk[l] = tall.T.astype(BF16)

    def rates(l, s, normed):
        both = dot(normed, rk[l]).T
        z = jnp.where(core == 0, both[0:heads], both[heads : 2 * heads])
        z = z + jnp.concatenate([colc[l, 0]] * (tokens // 128), axis=1)
        e = jnp.exp(-jnp.abs(z))
        small = e * (1.0 - e * (0.5 - e * (1.0 / 3.0 - e * 0.25)))
        step = jnp.maximum(z, 0.0) + jnp.where(e < 0.01, small, jnp.log(1.0 + e))
        ld = -step * jnp.concatenate([colc[l, 1]] * (tokens // 128), axis=1)
        hi = ld.astype(BF16)
        mid, lo = split2(ld - hi.astype(F32))
        c3 = dot(jnp.concatenate([hi, mid, lo], axis=0), triu[...])
        c = c3[0:heads] + c3[heads : 2 * heads] + c3[2 * heads : 3 * heads]
        r = c - jnp.log(step) * LOG2E
        rowt[s] = r
        last = jnp.broadcast_to(c[:, tokens - 1 : tokens], (heads, tokens))
        tail = jnp.exp2(last - r)
        thi = tail.astype(BF16).astype(F32)
        grown = jnp.exp2(c)
        ghi = grown.astype(BF16).astype(F32)
        stack = [c, thi, tail - thi, ghi, grown - ghi, jnp.zeros((128 - 5 * heads, tokens), F32)]
        col = jnp.concatenate(stack, axis=0).T
        cum[s] = col
        narrow = col.astype(BF16)
        cols16[s] = narrow
        d = jnp.exp2(last[:, 0:128])
        dhi = d.astype(BF16).astype(F32)
        dk[s, 0:heads] = dhi
        dk[s, heads : 2 * heads] = d - dhi

    def front_both():
        embed.wait()
        columns(0)
        span = edge_rows + tokens
        for s in range(seqs):
            normed = normalize(0, h[0, s])
            nx[span * s + edge_rows : span * (s + 1)] = normed
            rates(0, s, normed)

        @pl.when(me > 0)
        def _():
            edge_copy(me).wait_recv()

        @pl.when(me == 0)
        def _():
            edge[...] = jnp.zeros_like(edge)

        for s in range(seqs):
            nx[span * s : span * s + edge_rows] = normalize(0, edge[s])
        for j in range(chunks):
            ready(0, [j])
            made = dot(nx[...], win[0, :, cols * j : cols * (j + 1)])
            for s in range(seqs):
                xs[0, s, :, cols * j : cols * (j + 1)] = made[span * (s + 1) - tokens - 8 : span * (s + 1)]

    def front(s):
        normed = normalize(1, h[1, s])
        for lo in range(0, half + bc, cols):
            xs[1, s, 8 : 8 + tokens, lo : lo + cols] = dot(normed, win[1, :, lo : lo + cols])

        @pl.when(me < blocks - 1)
        def _():
            halo_copy(s, me + 1).start()

        rates(1, s, normed)

    def convolved(l, s, lo):
        if lo < half:
            col = pl.ds(pl.multiple_of(core * half + lo, 128), 128)
        else:
            col = pl.ds(inner + lo - half, 128)
        acc = tb[l, :, col] + xs[l, s, 8 : 8 + tokens, lo : lo + 128] * tp[l, 3:4, col]
        for k in range(3):
            acc = acc + xs[l, s, 5 + k : 5 + k + tokens, lo : lo + 128] * tp[l, k : k + 1, col]
        a = 0.5 * acc
        v = (a + a * jnp.tanh(a)).astype(BF16)
        act[s, :, lo : lo + 128] = v
        return v

    def middle(l, s):
        if l == 1:
            @pl.when(me > 0)
            def _():
                halo_copy(s, me).wait_recv()
                xs[1, s, 0:8, :] = halo[s]

            @pl.when(me == 0)
            def _():
                xs[1, s, 0:8, :] = jnp.zeros((8, half + bc), F32)

        bt = convolved(l, s, half).astype(F32).T.astype(BF16)
        per = 256 // head
        for j in range(half // 256):
            lo = 256 * j
            v = jnp.concatenate([convolved(l, s, lo), convolved(l, s, lo + 128)], axis=1)
            weighted = (v.astype(F32) * dot(cols16[s], expand[:, lo : lo + 256])).astype(BF16)
            state = dot(bt, weighted).T.astype(BF16)
            for q in range(per):
                hd = per * j + q
                msg[l, s, hd, 0:head, :] = state[head * q : head * (q + 1), :]
                both = [jnp.broadcast_to(dk[s, i : i + 1, :], (8, 128)) for i in (hd, heads + hd)]
                msg[l, s, hd, head : head + DECAY_ROWS, :] = jnp.concatenate(both, axis=0).astype(BF16)

            def send(b, _):
                @pl.when(b != me)
                def _():
                    state_copy(l, s, b).start()

                return 0

            lax.fori_loop(per * j, per * (j + 1), send, 0)

    def diagonal(l, s):
        hr = tokens // 2
        b = act[s, :, half : half + nstate]
        c = convolved(l, s, half + nstate)
        scores[...] = dot_nt(c, b)
        mask = lax.broadcasted_iota(jnp.int32, (hr, hr), 0) >= lax.broadcasted_iota(jnp.int32, (hr, hr), 1)
        lane = lax.broadcasted_iota(jnp.int32, (tokens, 128), 1) < head
        sk = mine(sg[l])
        for j in range(half // 128):
            lo = 128 * j
            vals = act[s, :, lo : lo + 128]
            zero = jnp.zeros_like(vals)
            gain = jnp.where(
                lane[0:1], jnp.broadcast_to(sk[:, 2 * j : 2 * j + 1], (1, 128)),
                jnp.broadcast_to(sk[:, 2 * j + 1 : 2 * j + 2], (1, 128)),
            )
            top = vals[0:hr].astype(F32) * gain
            bot = vals[hr:].astype(F32) * gain
            for q in range(2):
                hd = 2 * j + q
                v = jnp.where(lane, vals, zero) if q == 0 else jnp.where(lane, zero, vals)
                ct = jnp.broadcast_to(cum[s, 0:hr, hd : hd + 1], (hr, hr))
                cb = jnp.broadcast_to(cum[s, hr:tokens, hd : hd + 1], (hr, hr))
                r0 = rowt[s, hd : hd + 1, 0:hr]
                r1 = rowt[s, hd : hd + 1, hr:tokens]
                m00 = jnp.where(mask, jnp.exp2(ct - r0) * scores[0:hr, 0:hr], 0.0).astype(BF16)
                m10 = (jnp.exp2(cb - r0) * scores[hr:tokens, 0:hr]).astype(BF16)
                m11 = jnp.where(mask, jnp.exp2(cb - r1) * scores[hr:tokens, hr:tokens], 0.0).astype(BF16)
                top = top + dot(m00, v[0:hr])
                bot = bot + dot(jnp.concatenate([m10, m11], axis=1), v)
            total[s, 0:hr, lo : lo + 128] = top
            total[s, hr:tokens, lo : lo + 128] = bot

    def scan(l, s):
        rcv[l, s, me] = msg[l, s, me]

        def step(b, state):
            @pl.when(b != me)
            def _():
                state_arrival(l, s, b).wait_recv()

            inco[l, s, b] = state.astype(BF16)

            @pl.when(b != me)
            def _():
                reply_copy(l, s, b).start()

            m = rcv[l, s, b].astype(F32)
            d = m[head : head + 8] + m[head + 8 : head + 16]
            return state * jnp.concatenate([d] * (head // 8), axis=0) + m[0:head]

        lax.fori_loop(0, blocks, step, jnp.zeros((head, nstate), F32))
        inc[l, s, me] = inco[l, s, me]

    def back(l, s):
        def arrive(b, _):
            @pl.when(b != me)
            def _():
                reply_arrival(l, s, b).wait_recv()

            return 0

        c = act[s, :, half + nstate : half + bc]
        grown = cols16[s]
        sq = jnp.zeros((tokens, 1), F32)
        ys = []
        per = 256 // head
        for j in range(half // 256):
            lo = 256 * j
            lax.fori_loop(per * j, per * (j + 1), arrive, 0)
            incoming = inc[l, s, per * j : per * (j + 1)].reshape(256, nstate)
            e = dot(grown, expand[:, half + lo : half + lo + 256])
            t = total[s, :, lo : lo + 256] + dot_nt(c, incoming) * e
            sq = sq + jnp.sum(t * t, axis=-1, keepdims=True)
            gain = ig[l, :, pl.ds(pl.multiple_of(core * half + lo, 256), 256)]
            ys.append((t * gain).astype(BF16))
        y = jnp.concatenate(ys, axis=1)
        shi = sq.astype(BF16).astype(F32)
        first = lax.broadcasted_iota(jnp.int32, (tokens, 128), 1) < 64
        part[l, s, :, 0:128] = jnp.where(first, shi, sq - shi).astype(BF16)
        for i, lo in enumerate(range(0, width, cols)):
            part[l, s, :, 128 + lo : 128 + lo + cols] = dot(y, wo[l, :, lo : lo + cols]).astype(BF16)
            if l == 0:
                part_copy(l, s, i).start()
            else:
                pl.when(core == 0)(part_copy(l, s, i).start)

    def finish(l, s, store):
        for i in range(width // cols):
            part_copy(l, s, i).wait_recv()
            if i == 0:
                sq = 0.0
                for at in (0, 64):
                    sq = sq + part[l, s, :, at : at + 1].astype(F32) + prec[l, s, :, at : at + 1].astype(F32)
                scale = jnp.broadcast_to(lax.rsqrt(sq * (1.0 / inner) + EPS), (tokens, 128))
            for lo in range(cols * i, cols * (i + 1), 128):
                at = slice(128 + lo, 256 + lo)
                y = part[l, s, :, at].astype(F32) + prec[l, s, :, at].astype(F32)
                new = h[l, s, :, lo : lo + 128].astype(F32) + y * scale
                store(lo, new.astype(BF16))

    def hidden_store(s):
        def store(lo, new):
            h[1, s, :, lo : lo + 128] = new

        return store

    def result_store(s):
        def store(lo, new):
            out[0, s, :, lo : lo + 128] = new

        return store

    def each(run):
        def body(s, _):
            run(s)
            return 0

        lax.fori_loop(0, seqs, body, 0)

    def exchange(l):
        each(lambda s: middle(l, s))
        if l == 0:
            pushes[-1].start()
            columns(1)
        else:
            @pl.when(core == 0)
            def _():
                out[0] = h[1]
        each(lambda s: (diagonal(l, s), scan(l, s)))
        ready(l, [count - 1])
        each(lambda s: back(l, s))

    front_both()
    exchange(0)
    ready(1, range(chunks))
    each(lambda s: (finish(0, s, hidden_store(s)), front(s)))
    exchange(1)

    @pl.when(core == 1)
    def _():
        each(lambda s: finish(1, s, result_store(s)))

    for copy in pushes:
        copy.wait_send()

    @pl.when(me < blocks - 1)
    def _():
        edge_copy(me + 1).wait_send()
        for s in range(seqs):
            halo_copy(s, me + 1).wait_send()

    for s in range(seqs):
        for i in range(width // cols):
            part_copy(0, s, i).wait_send()
            pl.when(core == 0)(part_copy(1, s, i).wait_send)

    def drain(k, _):
        for l in range(2):
            for s in range(seqs):
                peer = lax.rem(me + k, blocks)
                state_copy(l, s, peer).wait_send()
                reply_copy(l, s, peer).wait_send()
        return 0

    lax.fori_loop(1, blocks, drain, 0)


def shards(emb, wide, rate, taps, tbias, sbias, dlog, skip, ngain, igain, proj):
    blocks = lax.axis_size("block")
    seqs, tokens, width = emb.shape
    xbc = wide.shape[2]
    inner = proj.shape[1]
    half = inner // 2
    bc = xbc - inner
    heads = sbias.shape[1] // 2
    head = half // heads
    nstate = bc // 2
    assert heads == blocks and lax.axis_size("section") == 2
    hbm = pl.BlockSpec(memory_space=pltpu.HBM)
    operands = (emb, wide, jnp.swapaxes(rate, 1, 2), taps, tbias, sbias, dlog, skip, ngain, igain, proj)
    operands = [pltpu.with_memory_space_constraint(x, pltpu.HBM) for x in operands]
    V, dma = pltpu.VMEM, pltpu.SemaphoreType.DMA
    moved = (half + bc) // 256 + 9
    return pl.pallas_call(
        functools.partial(kernel, blocks),
        out_shape=jax.ShapeDtypeStruct((1, seqs, tokens, width), BF16),
        in_specs=[hbm] * 11,
        out_specs=pl.BlockSpec(memory_space=pltpu.VMEM),
        scratch_shapes=[
            V((2, seqs, tokens, width), BF16),
            V((seqs, 16, width), BF16),
            V((seqs * (tokens + 16), width), BF16),
            V((2, width, half + bc), BF16),
            V((2, half, width), BF16),
            V((2, 2 * heads, width), BF16),
            V((2, width, 128), BF16),
            V((2, 4, xbc), F32),
            V((2, 1, xbc), F32),
            V((2, 1, 2 * heads), F32),
            V((2, 1, 2 * heads), F32),
            V((2, 1, 2 * heads), F32),
            V((2, 1, width), F32),
            V((2, 1, inner), F32),
            V((tokens, tokens), BF16),
            V((128, 2 * half), BF16),
            V((2, 2, heads, 128), F32),
            V((2, seqs, tokens + 8, half + bc), F32),
            V((seqs, 8, half + bc), F32),
            V((seqs, tokens, half + bc), BF16),
            V((tokens, tokens), F32),
            V((seqs, tokens, 128), F32),
            V((seqs, tokens, 128), BF16),
            V((seqs, heads, tokens), F32),
            V((seqs, 2 * heads, 128), F32),
            V((seqs, tokens, half), F32),
            V((2, seqs, blocks, head + DECAY_ROWS, nstate), BF16),
            V((2, seqs, blocks, head + DECAY_ROWS, nstate), BF16),
            V((2, seqs, blocks, head, nstate), BF16),
            V((2, seqs, blocks, head, nstate), BF16),
            V((2, seqs, tokens, width + 128), BF16),
            V((2, seqs, tokens, width + 128), BF16),
            dma((moved + 1,)), dma((moved,)), dma((moved,)), dma(()), dma(()),
            dma((seqs,)), dma((seqs,)),
            dma((2, seqs, blocks)), dma((2, seqs, blocks)),
            dma((2, seqs, blocks)), dma((2, seqs, blocks)),
            dma((2, seqs, width // 256)), dma((2, seqs, width // 256)),
        ],
        compiler_params=pltpu.CompilerParams(
            collective_id=0, has_side_effects=True, vmem_limit_bytes=52 * 1024 * 1024
        ),
    )(*operands)


def solution(mesh):
    placed = (
        P("dp", "block", None),
        P("section", None, None),
        P("section", None, None),
        P("section", None, None),
        P("section", None),
        P("section", None),
        P("section", None),
        P("section", None),
        P("section", None),
        P("section", None),
        P("section", None, None),
    )
    return jax.shard_map(
        shards,
        mesh=mesh,
        in_specs=placed,
        out_specs=P("section", "dp", "block", None),
        check_vma=False,
    )
```

```python
import functools

import jax
import jax.numpy as jnp
from jax import lax
from jax.experimental import pallas as pl
from jax.experimental.pallas import tpu as pltpu
from jax.sharding import PartitionSpec as P

MESH = pl.DeviceIdType.MESH
F32, BF16 = jnp.float32, jnp.bfloat16
LOG2E = 1.4426950408889634
EPS = 1e-05
DECAY_ROWS = 16


def split2(x):
    hi = x.astype(BF16)
    return hi, (x - hi.astype(F32)).astype(BF16)


def dot(a, b):
    return jnp.dot(a, b, preferred_element_type=F32)


def dot_nt(a, b):
    return lax.dot_general(a, b, (((1,), (1,)), ((), ())), preferred_element_type=F32)


def kernel(
    blocks,
    emb, wide, rate, taps, tbias, sbias, dlog, skip, ngain, igain, proj,
    out,
    h, edge, nx, win, wo, rt, rk, tp, tb, sb, dl, sg, ng, ig, triu, expand, colc,
    xs, halo, act, scores, cum, cols16, rowt, dk, total,
    msg, rcv, inco, inc, part, prec,
    local_sem, wsend, wrecv, esend, erecv, hsend, hrecv,
    msend, mrecv, isend, irecv, psend, precv,
):
    core = lax.axis_index("section")
    me = lax.axis_index("block")
    other = 1 - core
    seqs, tokens, width = emb.shape
    half = wo.shape[1]
    bc = win.shape[2] - half
    nstate = bc // 2
    heads = msg.shape[2]
    head = half // heads
    inner = 2 * half
    edge_rows = edge.shape[1]
    cols = 256
    chunks = (half + bc) // cols
    pieces = [(0 if lo == 0 else lo + 128, lo + 128 + cols) for lo in range(0, width, cols)]

    barrier = pltpu.get_barrier_semaphore()
    pl.semaphore_signal(barrier, inc=1, device_id={"section": other}, device_id_type=MESH)

    def greet(k, _):
        peer = lax.rem(me + k, blocks)
        pl.semaphore_signal(barrier, inc=1, device_id={"block": peer}, device_id_type=MESH)
        return 0

    lax.fori_loop(1, blocks, greet, 0)

    def moves(which, layer):
        found = []
        for j in range(chunks):
            at = which * half + cols * j if cols * j < half else inner + cols * j - half
            found.append((wide.at[0, :, pl.ds(pl.multiple_of(at, cols), cols)], win.at[layer, :, pl.ds(cols * j, cols)]))
        found += [(rate.at[0], rt.at[layer]), (taps.at[0], tp.at[layer])]
        found += [(a, b.at[layer]) for a, b in ((tbias, tb), (sbias, sb), (dlog, dl), (skip, sg), (ngain, ng), (igain, ig))]
        found.append((proj.at[0, pl.ds(pl.multiple_of(which * half, half), half), :], wo.at[layer]))
        return found

    local = [pltpu.make_async_copy(a, b, local_sem.at[i]) for i, (a, b) in enumerate(moves(core, core))]
    count = len(local)
    embed = pltpu.make_async_copy(emb, h.at[0], local_sem.at[count])
    embed.start()
    for copy in local[chunks:-1] + local[:chunks] + local[-1:]:
        copy.start()

    def remote(i, move):
        return pltpu.make_async_remote_copy(
            src_ref=move[0], dst_ref=move[1], send_sem=wsend.at[i], recv_sem=wrecv.at[i],
            device_id={"section": other}, device_id_type=MESH,
        )

    pushes = [remote(i, m) for i, m in enumerate(moves(other, core))]
    arrivals = [remote(i, m) for i, m in enumerate(moves(core, other))]

    def edge_copy(peer):
        return pltpu.make_async_remote_copy(
            src_ref=emb.at[:, pl.ds(tokens - edge_rows, edge_rows), :], dst_ref=edge,
            send_sem=esend, recv_sem=erecv, device_id={"block": peer}, device_id_type=MESH,
        )

    pl.semaphore_wait(barrier, blocks)
    for copy in pushes[chunks:-1] + pushes[:chunks]:
        copy.start()

    @pl.when(me < blocks - 1)
    def _():
        edge_copy(me + 1).start()

    def ready(l, which):
        @pl.when(core == l)
        def _():
            for i in which:
                local[i].wait()

        @pl.when(core != l)
        def _():
            for i in which:
                arrivals[i].wait_recv()

    ri = lax.broadcasted_iota(jnp.int32, (tokens, tokens), 0)
    ci = lax.broadcasted_iota(jnp.int32, (tokens, tokens), 1)
    triu[...] = jnp.where(ri <= ci, 1.0, 0.0).astype(BF16)
    eh = lax.broadcasted_iota(jnp.int32, (heads, half), 0)
    ec = lax.broadcasted_iota(jnp.int32, (heads, half), 1)
    spread = jnp.where((ec >= eh * head) & (ec < eh * head + head), 1.0, 0.0).astype(BF16)
    expand[...] = jnp.zeros_like(expand)
    for i, lo in ((1, 0), (2, 0), (3, half), (4, half)):
        expand[heads * i : heads * (i + 1), lo : lo + half] = spread

    @pl.when(me == 0)
    def _():
        inc[...] = jnp.zeros_like(inc)

    def mine(row):
        return jnp.where(core == 0, row[:, 0:heads], row[:, heads : 2 * heads])

    def halo_copy(s, peer):
        return pltpu.make_async_remote_copy(
            src_ref=xs.at[1, s, pl.ds(tokens, 8), :], dst_ref=halo.at[s],
            send_sem=hsend.at[s], recv_sem=hrecv.at[s],
            device_id={"block": peer}, device_id_type=MESH,
        )

    def state_copy(l, s, b):
        return pltpu.make_async_remote_copy(
            src_ref=msg.at[l, s, b], dst_ref=rcv.at[l, s, me],
            send_sem=msend.at[l, s, b], recv_sem=mrecv.at[l, s, me],
            device_id={"block": b}, device_id_type=MESH,
        )

    def state_arrival(l, s, b):
        return pltpu.make_async_remote_copy(
            src_ref=msg.at[l, s, b], dst_ref=rcv.at[l, s, b],
            send_sem=msend.at[l, s, b], recv_sem=mrecv.at[l, s, b],
            device_id={"block": b}, device_id_type=MESH,
        )

    def reply_copy(l, s, b):
        return pltpu.make_async_remote_copy(
            src_ref=inco.at[l, s, b], dst_ref=inc.at[l, s, me],
            send_sem=isend.at[l, s, b], recv_sem=irecv.at[l, s, me],
            device_id={"block": b}, device_id_type=MESH,
        )

    def reply_arrival(l, s, b):
        return pltpu.make_async_remote_copy(
            src_ref=inco.at[l, s, b], dst_ref=inc.at[l, s, b],
            send_sem=isend.at[l, s, b], recv_sem=irecv.at[l, s, b],
            device_id={"block": b}, device_id_type=MESH,
        )

    def part_copy(l, s, i):
        at = pl.ds(pieces[i][0], pieces[i][1] - pieces[i][0])
        return pltpu.make_async_remote_copy(
            src_ref=part.at[l, s, :, at], dst_ref=prec.at[l, s, :, at],
            send_sem=psend.at[l, s, i], recv_sem=precv.at[l, s, i],
            device_id={"section": other}, device_id_type=MESH,
        )

    def normalize(l, x):
        x = x.astype(F32)
        mean = jnp.mean(x * x, axis=-1, keepdims=True)
        return (x * lax.rsqrt(mean + EPS) * ng[l]).astype(BF16)

    def columns(l):
        ready(l, range(chunks, count - 1))
        for i, row in ((0, mine(sb[l])), (1, jnp.exp(mine(dl[l])) * LOG2E)):
            wide_row = jnp.concatenate([row, jnp.zeros((1, 128 - heads), F32)], axis=1)
            colc[l, i] = jnp.broadcast_to(wide_row, (128, 128)).T[0:heads]
        tall = jnp.concatenate([rt[l].astype(F32), jnp.zeros((128 - 2 * heads, width), F32)], axis=0)
        rk[l] = tall.T.astype(BF16)

    def rates(l, s, normed):
        both = dot(normed, rk[l]).T
        z = jnp.where(core == 0, both[0:heads], both[heads : 2 * heads])
        z = z + jnp.concatenate([colc[l, 0]] * (tokens // 128), axis=1)
        e = jnp.exp(-jnp.abs(z))
        small = e * (1.0 - e * (0.5 - e * (1.0 / 3.0 - e * 0.25)))
        step = jnp.maximum(z, 0.0) + jnp.where(e < 0.01, small, jnp.log(1.0 + e))
        ld = -step * jnp.concatenate([colc[l, 1]] * (tokens // 128), axis=1)
        hi = ld.astype(BF16)
        mid, lo = split2(ld - hi.astype(F32))
        c3 = dot(jnp.concatenate([hi, mid, lo], axis=0), triu[...])
        c = c3[0:heads] + c3[heads : 2 * heads] + c3[2 * heads : 3 * heads]
        r = c - jnp.log(step) * LOG2E
        rowt[s] = r
        last = jnp.broadcast_to(c[:, tokens - 1 : tokens], (heads, tokens))
        tail = jnp.exp2(last - r)
        thi = tail.astype(BF16).astype(F32)
        grown = jnp.exp2(c)
        ghi = grown.astype(BF16).astype(F32)
        stack = [c, thi, tail - thi, ghi, grown - ghi, jnp.zeros((128 - 5 * heads, tokens), F32)]
        col = jnp.concatenate(stack, axis=0).T
        cum[s] = col
        narrow = col.astype(BF16)
        cols16[s] = narrow
        d = jnp.exp2(last[:, 0:128])
        dhi = d.astype(BF16).astype(F32)
        dk[s, 0:heads] = dhi
        dk[s, heads : 2 * heads] = d - dhi

    def front_both():
        embed.wait()
        columns(0)
        span = edge_rows + tokens
        for s in range(seqs):
            normed = normalize(0, h[0, s])
            nx[span * s + edge_rows : span * (s + 1)] = normed
            rates(0, s, normed)

        @pl.when(me > 0)
        def _():
            edge_copy(me).wait_recv()

        @pl.when(me == 0)
        def _():
            edge[...] = jnp.zeros_like(edge)

        for s in range(seqs):
            nx[span * s : span * s + edge_rows] = normalize(0, edge[s])
        for j in range(chunks):
            ready(0, [j])
            made = dot(nx[...], win[0, :, cols * j : cols * (j + 1)])
            for s in range(seqs):
                xs[0, s, :, cols * j : cols * (j + 1)] = made[span * (s + 1) - tokens - 8 : span * (s + 1)]

    def front(s):
        normed = normalize(1, h[1, s])
        for lo in range(0, half + bc, cols):
            xs[1, s, 8 : 8 + tokens, lo : lo + cols] = dot(normed, win[1, :, lo : lo + cols])

        @pl.when(me < blocks - 1)
        def _():
            halo_copy(s, me + 1).start()

        rates(1, s, normed)

    def convolved(l, s, lo):
        if lo < half:
            col = pl.ds(pl.multiple_of(core * half + lo, 128), 128)
        else:
            col = pl.ds(inner + lo - half, 128)
        acc = tb[l, :, col] + xs[l, s, 8 : 8 + tokens, lo : lo + 128] * tp[l, 3:4, col]
        for k in range(3):
            acc = acc + xs[l, s, 5 + k : 5 + k + tokens, lo : lo + 128] * tp[l, k : k + 1, col]
        a = 0.5 * acc
        v = (a + a * jnp.tanh(a)).astype(BF16)
        act[s, :, lo : lo + 128] = v
        return v

    def middle(l, s):
        if l == 1:
            @pl.when(me > 0)
            def _():
                halo_copy(s, me).wait_recv()
                xs[1, s, 0:8, :] = halo[s]

            @pl.when(me == 0)
            def _():
                xs[1, s, 0:8, :] = jnp.zeros((8, half + bc), F32)

        bt = convolved(l, s, half).astype(F32).T.astype(BF16)
        per = 256 // head
        for j in range(half // 256):
            lo = 256 * j
            v = jnp.concatenate([convolved(l, s, lo), convolved(l, s, lo + 128)], axis=1)
            weighted = (v.astype(F32) * dot(cols16[s], expand[:, lo : lo + 256])).astype(BF16)
            state = dot(bt, weighted).T.astype(BF16)
            for q in range(per):
                hd = per * j + q
                msg[l, s, hd, 0:head, :] = state[head * q : head * (q + 1), :]
                both = [jnp.broadcast_to(dk[s, i : i + 1, :], (DECAY_ROWS // 2, 128)) for i in (hd, heads + hd)]
                msg[l, s, hd, head : head + DECAY_ROWS, :] = jnp.concatenate(both, axis=0).astype(BF16)

            def send(b, _):
                @pl.when((b != me) & (me < blocks - 1))
                def _():
                    state_copy(l, s, b).start()

                return 0

            lax.fori_loop(per * j, per * (j + 1), send, 0)

    def diagonal(l, s):
        hr = tokens // 2
        b = act[s, :, half : half + nstate]
        c = convolved(l, s, half + nstate)
        scores[...] = dot_nt(c, b)
        mask = lax.broadcasted_iota(jnp.int32, (hr, hr), 0) >= lax.broadcasted_iota(jnp.int32, (hr, hr), 1)
        lane = lax.broadcasted_iota(jnp.int32, (tokens, 128), 1) < head
        sk = mine(sg[l])
        for j in range(half // 128):
            lo = 128 * j
            vals = act[s, :, lo : lo + 128]
            zero = jnp.zeros_like(vals)
            gain = jnp.where(
                lane[0:1], jnp.broadcast_to(sk[:, 2 * j : 2 * j + 1], (1, 128)),
                jnp.broadcast_to(sk[:, 2 * j + 1 : 2 * j + 2], (1, 128)),
            )
            top = vals[0:hr].astype(F32) * gain
            bot = vals[hr:].astype(F32) * gain
            for q in range(2):
                hd = 2 * j + q
                v = jnp.where(lane, vals, zero) if q == 0 else jnp.where(lane, zero, vals)
                ct = jnp.broadcast_to(cum[s, 0:hr, hd : hd + 1], (hr, hr))
                cb = jnp.broadcast_to(cum[s, hr:tokens, hd : hd + 1], (hr, hr))
                r0 = rowt[s, hd : hd + 1, 0:hr]
                r1 = rowt[s, hd : hd + 1, hr:tokens]
                m00 = jnp.where(mask, jnp.exp2(ct - r0) * scores[0:hr, 0:hr], 0.0).astype(BF16)
                m10 = (jnp.exp2(cb - r0) * scores[hr:tokens, 0:hr]).astype(BF16)
                m11 = jnp.where(mask, jnp.exp2(cb - r1) * scores[hr:tokens, hr:tokens], 0.0).astype(BF16)
                top = top + dot(m00, v[0:hr])
                bot = bot + dot(jnp.concatenate([m10, m11], axis=1), v)
            total[s, 0:hr, lo : lo + 128] = top
            total[s, hr:tokens, lo : lo + 128] = bot

    def scan(l, s):
        rcv[l, s, me] = msg[l, s, me]

        def reply(b, state):
            inco[l, s, b] = state.astype(BF16)

            @pl.when((b != me) & (b > 0))
            def _():
                reply_copy(l, s, b).start()

        def step(b, state):
            reply(b, state)

            @pl.when(b != me)
            def _():
                state_arrival(l, s, b).wait_recv()

            m = rcv[l, s, b].astype(F32)
            at = [head, head + DECAY_ROWS // 2]
            d = m[at[0] : at[0] + 1] + m[at[1] : at[1] + 1]
            return state * d + m[0:head]

        reply(blocks - 1, lax.fori_loop(0, blocks - 1, step, jnp.zeros((head, nstate), F32)))
        inc[l, s, me] = inco[l, s, me]

    def back(l, s):
        def arrive(b, _):
            @pl.when((b != me) & (me > 0))
            def _():
                reply_arrival(l, s, b).wait_recv()

            return 0

        c = act[s, :, half + nstate : half + bc]
        grown = cols16[s]
        sq = jnp.zeros((tokens, 1), F32)
        ys = []
        per = 256 // head
        for j in range(half // 256):
            lo = 256 * j
            lax.fori_loop(per * j, per * (j + 1), arrive, 0)
            incoming = inc[l, s, per * j : per * (j + 1)].reshape(256, nstate)
            e = dot(grown, expand[:, half + lo : half + lo + 256])
            t = total[s, :, lo : lo + 256] + dot_nt(c, incoming) * e
            sq = sq + jnp.sum(t * t, axis=-1, keepdims=True)
            gain = ig[l, :, pl.ds(pl.multiple_of(core * half + lo, 256), 256)]
            ys.append((t * gain).astype(BF16))
        y = jnp.concatenate(ys, axis=1)
        shi = sq.astype(BF16).astype(F32)
        first = lax.broadcasted_iota(jnp.int32, (tokens, 128), 1) < 64
        part[l, s, :, 0:128] = jnp.where(first, shi, sq - shi).astype(BF16)
        for i, lo in enumerate(range(0, width, cols)):
            part[l, s, :, 128 + lo : 128 + lo + cols] = dot(y, wo[l, :, lo : lo + cols]).astype(BF16)
            if l == 0:
                part_copy(l, s, i).start()
            else:
                pl.when(core == 0)(part_copy(l, s, i).start)

    def finish(l, s, store):
        for i in range(width // cols):
            part_copy(l, s, i).wait_recv()
            if i == 0:
                sq = 0.0
                for at in (0, 64):
                    sq = sq + part[l, s, :, at : at + 1].astype(F32) + prec[l, s, :, at : at + 1].astype(F32)
                scale = jnp.broadcast_to(lax.rsqrt(sq * (1.0 / inner) + EPS), (tokens, 128))
            for lo in range(cols * i, cols * (i + 1), 128):
                at = slice(128 + lo, 256 + lo)
                y = part[l, s, :, at].astype(F32) + prec[l, s, :, at].astype(F32)
                new = h[l, s, :, lo : lo + 128].astype(F32) + y * scale
                store(lo, new.astype(BF16))

    def hidden_store(s):
        def store(lo, new):
            h[1, s, :, lo : lo + 128] = new

        return store

    def result_store(s):
        def store(lo, new):
            out[0, s, :, lo : lo + 128] = new

        return store

    def each(run):
        def body(s, _):
            run(s)
            return 0

        lax.fori_loop(0, seqs, body, 0)

    def exchange(l):
        each(lambda s: middle(l, s))
        if l == 0:
            pushes[-1].start()
            columns(1)
        else:
            @pl.when(core == 0)
            def _():
                out[0] = h[1]
        each(lambda s: (diagonal(l, s), scan(l, s)))
        ready(l, [count - 1])
        each(lambda s: back(l, s))

    front_both()
    exchange(0)
    ready(1, range(chunks))
    each(lambda s: (finish(0, s, hidden_store(s)), front(s)))
    exchange(1)

    @pl.when(core == 1)
    def _():
        each(lambda s: finish(1, s, result_store(s)))

    for copy in pushes:
        copy.wait_send()

    @pl.when(me < blocks - 1)
    def _():
        edge_copy(me + 1).wait_send()
        for s in range(seqs):
            halo_copy(s, me + 1).wait_send()

    for s in range(seqs):
        for i in range(width // cols):
            part_copy(0, s, i).wait_send()
            pl.when(core == 0)(part_copy(1, s, i).wait_send)

    def drain(k, _):
        for l in range(2):
            for s in range(seqs):
                peer = lax.rem(me + k, blocks)
                pl.when(me < blocks - 1)(state_copy(l, s, peer).wait_send)
                pl.when(peer > 0)(reply_copy(l, s, peer).wait_send)
        return 0

    lax.fori_loop(1, blocks, drain, 0)


def shards(emb, wide, rate, taps, tbias, sbias, dlog, skip, ngain, igain, proj):
    blocks = lax.axis_size("block")
    seqs, tokens, width = emb.shape
    xbc = wide.shape[2]
    inner = proj.shape[1]
    half = inner // 2
    bc = xbc - inner
    heads = sbias.shape[1] // 2
    head = half // heads
    nstate = bc // 2
    assert heads == blocks and lax.axis_size("section") == 2
    hbm = pl.BlockSpec(memory_space=pltpu.HBM)
    operands = (emb, wide, jnp.swapaxes(rate, 1, 2), taps, tbias, sbias, dlog, skip, ngain, igain, proj)
    operands = [pltpu.with_memory_space_constraint(x, pltpu.HBM) for x in operands]
    V, dma = pltpu.VMEM, pltpu.SemaphoreType.DMA
    moved = (half + bc) // 256 + 9
    return pl.pallas_call(
        functools.partial(kernel, blocks),
        out_shape=jax.ShapeDtypeStruct((1, seqs, tokens, width), BF16),
        in_specs=[hbm] * 11,
        out_specs=pl.BlockSpec(memory_space=pltpu.VMEM),
        scratch_shapes=[
            V((2, seqs, tokens, width), BF16),
            V((seqs, 16, width), BF16),
            V((seqs * (tokens + 16), width), BF16),
            V((2, width, half + bc), BF16),
            V((2, half, width), BF16),
            V((2, 2 * heads, width), BF16),
            V((2, width, 128), BF16),
            V((2, 4, xbc), F32),
            V((2, 1, xbc), F32),
            V((2, 1, 2 * heads), F32),
            V((2, 1, 2 * heads), F32),
            V((2, 1, 2 * heads), F32),
            V((2, 1, width), F32),
            V((2, 1, inner), F32),
            V((tokens, tokens), BF16),
            V((128, 2 * half), BF16),
            V((2, 2, heads, 128), F32),
            V((2, seqs, tokens + 8, half + bc), F32),
            V((seqs, 8, half + bc), F32),
            V((seqs, tokens, half + bc), BF16),
            V((tokens, tokens), F32),
            V((seqs, tokens, 128), F32),
            V((seqs, tokens, 128), BF16),
            V((seqs, heads, tokens), F32),
            V((seqs, 2 * heads, 128), F32),
            V((seqs, tokens, half), F32),
            V((2, seqs, blocks, head + DECAY_ROWS, nstate), BF16),
            V((2, seqs, blocks, head + DECAY_ROWS, nstate), BF16),
            V((2, seqs, blocks, head, nstate), BF16),
            V((2, seqs, blocks, head, nstate), BF16),
            V((2, seqs, tokens, width + 128), BF16),
            V((2, seqs, tokens, width + 128), BF16),
            dma((moved + 1,)), dma((moved,)), dma((moved,)), dma(()), dma(()),
            dma((seqs,)), dma((seqs,)),
            dma((2, seqs, blocks)), dma((2, seqs, blocks)),
            dma((2, seqs, blocks)), dma((2, seqs, blocks)),
            dma((2, seqs, width // 256)), dma((2, seqs, width // 256)),
        ],
        compiler_params=pltpu.CompilerParams(
            collective_id=0, has_side_effects=True, vmem_limit_bytes=52 * 1024 * 1024
        ),
    )(*operands)


def solution(mesh):
    placed = (
        P("dp", "block", None),
        P("section", None, None),
        P("section", None, None),
        P("section", None, None),
        P("section", None),
        P("section", None),
        P("section", None),
        P("section", None),
        P("section", None),
        P("section", None),
        P("section", None, None),
    )
    return jax.shard_map(
        shards,
        mesh=mesh,
        in_specs=placed,
        out_specs=P("section", "dp", "block", None),
        check_vma=False,
    )
```

```python
import functools

import jax
import jax.numpy as jnp
from jax import lax
from jax.experimental import pallas as pl
from jax.experimental.pallas import tpu as pltpu
from jax.sharding import PartitionSpec as P

MESH = pl.DeviceIdType.MESH
F32, BF16 = jnp.float32, jnp.bfloat16
LOG2E = 1.4426950408889634
EPS = 1e-05
DECAY_ROWS = 16


def split2(x):
    hi = x.astype(BF16)
    return hi, (x - hi.astype(F32)).astype(BF16)


def dot(a, b):
    return jnp.dot(a, b, preferred_element_type=F32)


def dot_nt(a, b):
    return lax.dot_general(a, b, (((1,), (1,)), ((), ())), preferred_element_type=F32)


def kernel(
    blocks,
    emb, wide, rate, taps, tbias, sbias, dlog, skip, ngain, igain, proj,
    out,
    h, edge, nx, win, wo, rt, rk, tp, tb, sb, dl, sg, ng, ig, triu, expand, colc,
    xs, halo, act, scores, cum, cols16, rowt, dk, total,
    msg, rcv, inco, inc, part, prec,
    local_sem, wsend, wrecv, esend, erecv, hsend, hrecv,
    msend, mrecv, isend, irecv, psend, precv,
):
    core = lax.axis_index("section")
    me = lax.axis_index("block")
    other = 1 - core
    seqs, tokens, width = emb.shape
    half = wo.shape[1]
    bc = win.shape[2] - half
    nstate = bc // 2
    heads = msg.shape[2]
    head = half // heads
    inner = 2 * half
    edge_rows = edge.shape[1]
    cols = 256
    chunks = (half + bc) // cols
    pieces = [(0 if lo == 0 else lo + 128, lo + 128 + cols) for lo in range(0, width, cols)]

    barrier = pltpu.get_barrier_semaphore()
    pl.semaphore_signal(barrier, inc=1, device_id={"section": other}, device_id_type=MESH)

    def greet(k, _):
        peer = lax.rem(me + k, blocks)
        pl.semaphore_signal(barrier, inc=1, device_id={"block": peer}, device_id_type=MESH)
        return 0

    lax.fori_loop(1, blocks, greet, 0)

    def moves(which, layer):
        found = []
        for j in range(chunks):
            at = which * half + cols * j if cols * j < half else inner + cols * j - half
            found.append((wide.at[0, :, pl.ds(pl.multiple_of(at, cols), cols)], win.at[layer, :, pl.ds(cols * j, cols)]))
        found += [(rate.at[0], rt.at[layer]), (taps.at[0], tp.at[layer])]
        found += [(a, b.at[layer]) for a, b in ((tbias, tb), (sbias, sb), (dlog, dl), (skip, sg), (ngain, ng), (igain, ig))]
        found.append((proj.at[0, pl.ds(pl.multiple_of(which * half, half), half), :], wo.at[layer]))
        return found

    local = [pltpu.make_async_copy(a, b, local_sem.at[i]) for i, (a, b) in enumerate(moves(core, core))]
    count = len(local)
    embed = pltpu.make_async_copy(emb, h.at[0], local_sem.at[count])
    embed.start()
    for copy in local[chunks:-1] + local[:chunks] + local[-1:]:
        copy.start()

    def remote(i, move):
        return pltpu.make_async_remote_copy(
            src_ref=move[0], dst_ref=move[1], send_sem=wsend.at[i], recv_sem=wrecv.at[i],
            device_id={"section": other}, device_id_type=MESH,
        )

    pushes = [remote(i, m) for i, m in enumerate(moves(other, core))]
    arrivals = [remote(i, m) for i, m in enumerate(moves(core, other))]

    def edge_copy(peer):
        return pltpu.make_async_remote_copy(
            src_ref=emb.at[:, pl.ds(tokens - edge_rows, edge_rows), :], dst_ref=edge,
            send_sem=esend, recv_sem=erecv, device_id={"block": peer}, device_id_type=MESH,
        )

    pl.semaphore_wait(barrier, blocks)
    for copy in pushes[chunks:-1] + pushes[:chunks]:
        copy.start()

    @pl.when(me < blocks - 1)
    def _():
        edge_copy(me + 1).start()

    def ready(l, which):
        @pl.when(core == l)
        def _():
            for i in which:
                local[i].wait()

        @pl.when(core != l)
        def _():
            for i in which:
                arrivals[i].wait_recv()

    ri = lax.broadcasted_iota(jnp.int32, (tokens, tokens), 0)
    ci = lax.broadcasted_iota(jnp.int32, (tokens, tokens), 1)
    triu[...] = jnp.where(ri <= ci, 1.0, 0.0).astype(BF16)
    eh = lax.broadcasted_iota(jnp.int32, (heads, half), 0)
    ec = lax.broadcasted_iota(jnp.int32, (heads, half), 1)
    spread = jnp.where((ec >= eh * head) & (ec < eh * head + head), 1.0, 0.0).astype(BF16)
    expand[...] = jnp.zeros_like(expand)
    for i, lo in ((1, 0), (2, 0), (3, half), (4, half)):
        expand[heads * i : heads * (i + 1), lo : lo + half] = spread

    @pl.when(me == 0)
    def _():
        inc[...] = jnp.zeros_like(inc)

    def mine(row):
        return jnp.where(core == 0, row[:, 0:heads], row[:, heads : 2 * heads])

    def halo_copy(s, peer, i):
        at = pl.ds(*((0, 3 * cols), (3 * cols, half + bc - 3 * cols))[i])
        return pltpu.make_async_remote_copy(
            src_ref=xs.at[1, s, pl.ds(tokens, 8), at], dst_ref=halo.at[s, :, at],
            send_sem=hsend.at[s, i], recv_sem=hrecv.at[s, i],
            device_id={"block": peer}, device_id_type=MESH,
        )

    def state_copy(l, s, b):
        return pltpu.make_async_remote_copy(
            src_ref=msg.at[l, s, b], dst_ref=rcv.at[l, s, me],
            send_sem=msend.at[l, s, b], recv_sem=mrecv.at[l, s, me],
            device_id={"block": b}, device_id_type=MESH,
        )

    def state_arrival(l, s, b):
        return pltpu.make_async_remote_copy(
            src_ref=msg.at[l, s, b], dst_ref=rcv.at[l, s, b],
            send_sem=msend.at[l, s, b], recv_sem=mrecv.at[l, s, b],
            device_id={"block": b}, device_id_type=MESH,
        )

    def reply_copy(l, s, b):
        return pltpu.make_async_remote_copy(
            src_ref=inco.at[l, s, b], dst_ref=inc.at[l, s, me],
            send_sem=isend.at[l, s, b], recv_sem=irecv.at[l, s, me],
            device_id={"block": b}, device_id_type=MESH,
        )

    def reply_arrival(l, s, b):
        return pltpu.make_async_remote_copy(
            src_ref=inco.at[l, s, b], dst_ref=inc.at[l, s, b],
            send_sem=isend.at[l, s, b], recv_sem=irecv.at[l, s, b],
            device_id={"block": b}, device_id_type=MESH,
        )

    def part_copy(l, s, i):
        at = pl.ds(pieces[i][0], pieces[i][1] - pieces[i][0])
        return pltpu.make_async_remote_copy(
            src_ref=part.at[l, s, :, at], dst_ref=prec.at[l, s, :, at],
            send_sem=psend.at[l, s, i], recv_sem=precv.at[l, s, i],
            device_id={"section": other}, device_id_type=MESH,
        )

    def normalize(l, x):
        x = x.astype(F32)
        mean = jnp.mean(x * x, axis=-1, keepdims=True)
        return (x * lax.rsqrt(mean + EPS) * ng[l]).astype(BF16)

    def columns(l):
        ready(l, range(chunks, count - 1))
        for i, row in ((0, mine(sb[l])), (1, jnp.exp(mine(dl[l])) * LOG2E)):
            wide_row = jnp.concatenate([row, jnp.zeros((1, 128 - heads), F32)], axis=1)
            colc[l, i] = jnp.broadcast_to(wide_row, (128, 128)).T[0:heads]
        tall = jnp.concatenate([rt[l].astype(F32), jnp.zeros((128 - 2 * heads, width), F32)], axis=0)
        rk[l] = tall.T.astype(BF16)

    def rates(l, s, normed):
        both = dot(normed, rk[l]).T
        z = jnp.where(core == 0, both[0:heads], both[heads : 2 * heads])
        z = z + jnp.concatenate([colc[l, 0]] * (tokens // 128), axis=1)
        e = jnp.exp(-jnp.abs(z))
        small = e * (1.0 - e * (0.5 - e * (1.0 / 3.0 - e * 0.25)))
        step = jnp.maximum(z, 0.0) + jnp.where(e < 0.01, small, jnp.log(1.0 + e))
        ld = -step * jnp.concatenate([colc[l, 1]] * (tokens // 128), axis=1)
        hi = ld.astype(BF16)
        mid, lo = split2(ld - hi.astype(F32))
        c3 = dot(jnp.concatenate([hi, mid, lo], axis=0), triu[...])
        c = c3[0:heads] + c3[heads : 2 * heads] + c3[2 * heads : 3 * heads]
        r = c - jnp.log(step) * LOG2E
        rowt[s] = r
        last = jnp.broadcast_to(c[:, tokens - 1 : tokens], (heads, tokens))
        tail = jnp.exp2(last - r)
        thi = tail.astype(BF16).astype(F32)
        grown = jnp.exp2(c)
        ghi = grown.astype(BF16).astype(F32)
        stack = [c, thi, tail - thi, ghi, grown - ghi, jnp.zeros((128 - 5 * heads, tokens), F32)]
        col = jnp.concatenate(stack, axis=0).T
        cum[s] = col
        narrow = col.astype(BF16)
        cols16[s] = narrow
        d = jnp.exp2(last[:, 0:128])
        dhi = d.astype(BF16).astype(F32)
        dk[s, 0:heads] = dhi
        dk[s, heads : 2 * heads] = d - dhi

    def front_both():
        embed.wait()
        columns(0)
        span = edge_rows + tokens
        for s in range(seqs):
            normed = normalize(0, h[0, s])
            nx[span * s + edge_rows : span * (s + 1)] = normed
            rates(0, s, normed)

        @pl.when(me > 0)
        def _():
            edge_copy(me).wait_recv()

        @pl.when(me == 0)
        def _():
            edge[...] = jnp.zeros_like(edge)

        for s in range(seqs):
            nx[span * s : span * s + edge_rows] = normalize(0, edge[s])
        for j in range(chunks):
            ready(0, [j])
            made = dot(nx[...], win[0, :, cols * j : cols * (j + 1)])
            for s in range(seqs):
                xs[0, s, :, cols * j : cols * (j + 1)] = made[span * (s + 1) - tokens - 8 : span * (s + 1)]

    def front(s):
        normed = normalize(1, h[1, s])
        for lo in range(0, half + bc, cols):
            xs[1, s, 8 : 8 + tokens, lo : lo + cols] = dot(normed, win[1, :, lo : lo + cols])
            if lo == 2 * cols:
                pl.when(me < blocks - 1)(halo_copy(s, me + 1, 0).start)

        pl.when(me < blocks - 1)(halo_copy(s, me + 1, 1).start)

        rates(1, s, normed)

    def convolved(l, s, lo):
        if lo < half:
            col = pl.ds(pl.multiple_of(core * half + lo, 128), 128)
        else:
            col = pl.ds(inner + lo - half, 128)
        acc = tb[l, :, col] + xs[l, s, 8 : 8 + tokens, lo : lo + 128] * tp[l, 3:4, col]
        for k in range(3):
            acc = acc + xs[l, s, 5 + k : 5 + k + tokens, lo : lo + 128] * tp[l, k : k + 1, col]
        a = 0.5 * acc
        v = (a + a * jnp.tanh(a)).astype(BF16)
        act[s, :, lo : lo + 128] = v
        return v

    def middle(l, s):
        if l == 1:
            @pl.when(me > 0)
            def _():
                for i in range(2):
                    halo_copy(s, me, i).wait_recv()
                xs[1, s, 0:8, :] = halo[s]

            @pl.when(me == 0)
            def _():
                xs[1, s, 0:8, :] = jnp.zeros((8, half + bc), F32)

        bt = convolved(l, s, half).astype(F32).T.astype(BF16)
        per = 256 // head
        for j in range(half // 256):
            lo = 256 * j
            v = jnp.concatenate([convolved(l, s, lo), convolved(l, s, lo + 128)], axis=1)
            weighted = (v.astype(F32) * dot(cols16[s], expand[:, lo : lo + 256])).astype(BF16)
            state = dot(bt, weighted).T.astype(BF16)
            for q in range(per):
                hd = per * j + q
                msg[l, s, hd, 0:head, :] = state[head * q : head * (q + 1), :]
                both = [jnp.broadcast_to(dk[s, i : i + 1, :], (DECAY_ROWS // 2, 128)) for i in (hd, heads + hd)]
                msg[l, s, hd, head : head + DECAY_ROWS, :] = jnp.concatenate(both, axis=0).astype(BF16)

            def send(b, _):
                @pl.when((b != me) & (me < blocks - 1))
                def _():
                    state_copy(l, s, b).start()

                return 0

            lax.fori_loop(per * j, per * (j + 1), send, 0)

    def diagonal(l, s):
        hr = tokens // 2
        b = act[s, :, half : half + nstate]
        c = convolved(l, s, half + nstate)
        scores[...] = dot_nt(c, b)
        mask = lax.broadcasted_iota(jnp.int32, (hr, hr), 0) >= lax.broadcasted_iota(jnp.int32, (hr, hr), 1)
        lane = lax.broadcasted_iota(jnp.int32, (tokens, 128), 1) < head
        sk = mine(sg[l])
        for j in range(half // 128):
            lo = 128 * j
            vals = act[s, :, lo : lo + 128]
            zero = jnp.zeros_like(vals)
            gain = jnp.where(
                lane[0:1], jnp.broadcast_to(sk[:, 2 * j : 2 * j + 1], (1, 128)),
                jnp.broadcast_to(sk[:, 2 * j + 1 : 2 * j + 2], (1, 128)),
            )
            top = vals[0:hr].astype(F32) * gain
            bot = vals[hr:].astype(F32) * gain
            for q in range(2):
                hd = 2 * j + q
                v = jnp.where(lane, vals, zero) if q == 0 else jnp.where(lane, zero, vals)
                ct = jnp.broadcast_to(cum[s, 0:hr, hd : hd + 1], (hr, hr))
                cb = jnp.broadcast_to(cum[s, hr:tokens, hd : hd + 1], (hr, hr))
                r0 = rowt[s, hd : hd + 1, 0:hr]
                r1 = rowt[s, hd : hd + 1, hr:tokens]
                m00 = jnp.where(mask, jnp.exp2(ct - r0) * scores[0:hr, 0:hr], 0.0).astype(BF16)
                m10 = (jnp.exp2(cb - r0) * scores[hr:tokens, 0:hr]).astype(BF16)
                m11 = jnp.where(mask, jnp.exp2(cb - r1) * scores[hr:tokens, hr:tokens], 0.0).astype(BF16)
                top = top + dot(m00, v[0:hr])
                bot = bot + dot(jnp.concatenate([m10, m11], axis=1), v)
            total[s, 0:hr, lo : lo + 128] = top
            total[s, hr:tokens, lo : lo + 128] = bot

    def scan(l, s):
        rcv[l, s, me] = msg[l, s, me]

        def reply(b, state):
            inco[l, s, b] = state.astype(BF16)

            @pl.when((b != me) & (b > 0))
            def _():
                reply_copy(l, s, b).start()

        def step(b, state):
            reply(b, state)

            @pl.when(b != me)
            def _():
                state_arrival(l, s, b).wait_recv()

            m = rcv[l, s, b].astype(F32)
            at = [head, head + DECAY_ROWS // 2]
            d = m[at[0] : at[0] + 1] + m[at[1] : at[1] + 1]
            return state * d + m[0:head]

        reply(blocks - 1, lax.fori_loop(0, blocks - 1, step, jnp.zeros((head, nstate), F32)))
        inc[l, s, me] = inco[l, s, me]

    def back(l, s):
        def arrive(b, _):
            @pl.when((b != me) & (me > 0))
            def _():
                reply_arrival(l, s, b).wait_recv()

            return 0

        c = act[s, :, half + nstate : half + bc]
        grown = cols16[s]
        sq = jnp.zeros((tokens, 1), F32)
        ys = []
        per = 256 // head
        for j in range(half // 256):
            lo = 256 * j
            lax.fori_loop(per * j, per * (j + 1), arrive, 0)
            incoming = inc[l, s, per * j : per * (j + 1)].reshape(256, nstate)
            e = dot(grown, expand[:, half + lo : half + lo + 256])
            t = total[s, :, lo : lo + 256] + dot_nt(c, incoming) * e
            sq = sq + jnp.sum(t * t, axis=-1, keepdims=True)
            gain = ig[l, :, pl.ds(pl.multiple_of(core * half + lo, 256), 256)]
            ys.append((t * gain).astype(BF16))
        y = jnp.concatenate(ys, axis=1)
        shi = sq.astype(BF16).astype(F32)
        first = lax.broadcasted_iota(jnp.int32, (tokens, 128), 1) < 64
        part[l, s, :, 0:128] = jnp.where(first, shi, sq - shi).astype(BF16)
        for i, lo in enumerate(range(0, width, cols)):
            part[l, s, :, 128 + lo : 128 + lo + cols] = dot(y, wo[l, :, lo : lo + cols]).astype(BF16)
            if l == 0:
                part_copy(l, s, i).start()
            else:
                pl.when(core == 0)(part_copy(l, s, i).start)

    def finish(l, s, store):
        for i in range(width // cols):
            part_copy(l, s, i).wait_recv()
            if i == 0:
                sq = 0.0
                for at in (0, 64):
                    sq = sq + part[l, s, :, at : at + 1].astype(F32) + prec[l, s, :, at : at + 1].astype(F32)
                scale = jnp.broadcast_to(lax.rsqrt(sq * (1.0 / inner) + EPS), (tokens, 128))
            for lo in range(cols * i, cols * (i + 1), 128):
                at = slice(128 + lo, 256 + lo)
                y = part[l, s, :, at].astype(F32) + prec[l, s, :, at].astype(F32)
                new = h[l, s, :, lo : lo + 128].astype(F32) + y * scale
                store(lo, new.astype(BF16))

    def hidden_store(s):
        def store(lo, new):
            h[1, s, :, lo : lo + 128] = new

        return store

    def result_store(s):
        def store(lo, new):
            out[0, s, :, lo : lo + 128] = new

        return store

    def each(run):
        def body(s, _):
            run(s)
            return 0

        lax.fori_loop(0, seqs, body, 0)

    def exchange(l):
        each(lambda s: middle(l, s))
        if l == 0:
            pushes[-1].start()
            columns(1)
        else:
            @pl.when(core == 0)
            def _():
                out[0] = h[1]
        each(lambda s: (diagonal(l, s), scan(l, s)))
        ready(l, [count - 1])
        each(lambda s: back(l, s))

    front_both()
    exchange(0)
    ready(1, range(chunks))
    each(lambda s: (finish(0, s, hidden_store(s)), front(s)))
    exchange(1)

    @pl.when(core == 1)
    def _():
        each(lambda s: finish(1, s, result_store(s)))

    for copy in pushes:
        copy.wait_send()

    @pl.when(me < blocks - 1)
    def _():
        edge_copy(me + 1).wait_send()
        for s in range(seqs):
            for i in range(2):
                halo_copy(s, me + 1, i).wait_send()

    for s in range(seqs):
        for i in range(width // cols):
            part_copy(0, s, i).wait_send()
            pl.when(core == 0)(part_copy(1, s, i).wait_send)

    def drain(k, _):
        for l in range(2):
            for s in range(seqs):
                peer = lax.rem(me + k, blocks)
                pl.when(me < blocks - 1)(state_copy(l, s, peer).wait_send)
                pl.when(peer > 0)(reply_copy(l, s, peer).wait_send)
        return 0

    lax.fori_loop(1, blocks, drain, 0)


def shards(emb, wide, rate, taps, tbias, sbias, dlog, skip, ngain, igain, proj):
    blocks = lax.axis_size("block")
    seqs, tokens, width = emb.shape
    xbc = wide.shape[2]
    inner = proj.shape[1]
    half = inner // 2
    bc = xbc - inner
    heads = sbias.shape[1] // 2
    head = half // heads
    nstate = bc // 2
    assert heads == blocks and lax.axis_size("section") == 2
    hbm = pl.BlockSpec(memory_space=pltpu.HBM)
    operands = (emb, wide, jnp.swapaxes(rate, 1, 2), taps, tbias, sbias, dlog, skip, ngain, igain, proj)
    operands = [pltpu.with_memory_space_constraint(x, pltpu.HBM) for x in operands]
    V, dma = pltpu.VMEM, pltpu.SemaphoreType.DMA
    moved = (half + bc) // 256 + 9
    return pl.pallas_call(
        functools.partial(kernel, blocks),
        out_shape=jax.ShapeDtypeStruct((1, seqs, tokens, width), BF16),
        in_specs=[hbm] * 11,
        out_specs=pl.BlockSpec(memory_space=pltpu.VMEM),
        scratch_shapes=[
            V((2, seqs, tokens, width), BF16),
            V((seqs, 16, width), BF16),
            V((seqs * (tokens + 16), width), BF16),
            V((2, width, half + bc), BF16),
            V((2, half, width), BF16),
            V((2, 2 * heads, width), BF16),
            V((2, width, 128), BF16),
            V((2, 4, xbc), F32),
            V((2, 1, xbc), F32),
            V((2, 1, 2 * heads), F32),
            V((2, 1, 2 * heads), F32),
            V((2, 1, 2 * heads), F32),
            V((2, 1, width), F32),
            V((2, 1, inner), F32),
            V((tokens, tokens), BF16),
            V((128, 2 * half), BF16),
            V((2, 2, heads, 128), F32),
            V((2, seqs, tokens + 8, half + bc), F32),
            V((seqs, 8, half + bc), F32),
            V((seqs, tokens, half + bc), BF16),
            V((tokens, tokens), F32),
            V((seqs, tokens, 128), F32),
            V((seqs, tokens, 128), BF16),
            V((seqs, heads, tokens), F32),
            V((seqs, 2 * heads, 128), F32),
            V((seqs, tokens, half), F32),
            V((2, seqs, blocks, head + DECAY_ROWS, nstate), BF16),
            V((2, seqs, blocks, head + DECAY_ROWS, nstate), BF16),
            V((2, seqs, blocks, head, nstate), BF16),
            V((2, seqs, blocks, head, nstate), BF16),
            V((2, seqs, tokens, width + 128), BF16),
            V((2, seqs, tokens, width + 128), BF16),
            dma((moved + 1,)), dma((moved,)), dma((moved,)), dma(()), dma(()),
            dma((seqs, 2)), dma((seqs, 2)),
            dma((2, seqs, blocks)), dma((2, seqs, blocks)),
            dma((2, seqs, blocks)), dma((2, seqs, blocks)),
            dma((2, seqs, width // 256)), dma((2, seqs, width // 256)),
        ],
        compiler_params=pltpu.CompilerParams(
            collective_id=0, has_side_effects=True, vmem_limit_bytes=52 * 1024 * 1024
        ),
    )(*operands)


def solution(mesh):
    placed = (
        P("dp", "block", None),
        P("section", None, None),
        P("section", None, None),
        P("section", None, None),
        P("section", None),
        P("section", None),
        P("section", None),
        P("section", None),
        P("section", None),
        P("section", None),
        P("section", None, None),
    )
    return jax.shard_map(
        shards,
        mesh=mesh,
        in_specs=placed,
        out_specs=P("section", "dp", "block", None),
        check_vma=False,
    )
```
